512 devices in a mesh: cam: 32 (over y, x_hi, core), head: 16 (over x_lo, z).
Axes of the slice: x: 4 (x_hi: 2, x_lo: 2; x = x_hi * 2 + x_lo), y: 8, z: 8, core: 2. Of those that a mesh axis runs over, the one named last changes fastest.
Arguments:
- queries: bfloat16 [65536, 4096], P('cam', 'head'), may hold values from -24 to 24
- keys: bfloat16 [65536, 4096], P('cam', 'head'), may hold values from -24 to 24
- values: bfloat16 [65536, 4096], P('cam', 'head'), may hold values from -6 to 6
- rates: float32 [65536, 16], P('cam', 'head'), may hold values from 0.1 to 1
- w_one: bfloat16 [16, 256, 256], P('head'), may hold values from -0.375 to 0.375
- w_three: bfloat16 [16, 256, 256], P('head'), may hold values from -0.375 to 0.375
- w_two: bfloat16 [16, 256, 256], P('head'), may hold values from -0.375 to 0.375
- gain: float32 [4096], P('head'), may hold values from 0.5 to 1.5
- order: int32 [32, 2048], P('cam'), may hold values from 0 to 2047, as said below
Outputs:
- mixed: bfloat16 [65536, 4096], P('cam', 'head')
The draws below stay inside these ranges and needn't reach their ends.
Inputs may be any that keep to these rules, and one draw needn't show every extreme that they name: `order`: each row is an ordering of 0 to 2047; every timestamp holds exactly 32 tokens of every camera.
All inputs are finite; a program needn't handle non-finite values.
Results may differ from the reference program's by a relative error of at most 0.0085.
Values may be sent and summed in bfloat16 or wider, within the bound.
A program may use at most 64 MiB of HBM per device.

```python
import math
import jax
import jax.numpy as jnp
from jax import lax

HD = 256
HID = 256
FRAMES = 64
PATCHES = 32
HEADS = 16
D = 4096
CAMERAS = 32
TOK_DEV = 2048
TOKENS = 65536


def order_table(key):
    keys_all = jax.random.split(jax.random.fold_in(key, 11), CAMERAS)
    table = jax.vmap(lambda single: jax.random.permutation(single, TOK_DEV))(keys_all)
    return table.astype(jnp.int32)


def paired_draw(key, which):
    own_key = jax.random.fold_in(key, 20 + which)
    result = jnp.clip(jax.random.normal(own_key, (CAMERAS, TOK_DEV, D), jnp.float32), -6.0, 6.0)
    return result.reshape(TOKENS, D).astype(jnp.bfloat16)


def draw_queries(key, part):
    return paired_draw(key, 0)


def draw_keys(key, part):
    return paired_draw(key, 1)


def draw_order(key, part):
    return order_table(key)


def block_scale(stream_key, shape, cuts, least, largest):
    def one(axis_at, blocks):
        steps = jax.random.uniform(jax.random.fold_in(jax.random.fold_in(stream_key, 6), axis_at), (blocks,), jnp.float32, least / len(cuts), largest / len(cuts))
        return jnp.repeat(jnp.exp(steps), shape[axis_at] // blocks).reshape((-1,) + (1,) * (len(shape) - axis_at - 1))

    factor_of = one(*cuts[0])
    for cut in cuts[1:]:
        factor_of = factor_of * one(*cut)
    return factor_of


def normal_values(key, shape, width, most, pieces=(), kind=jnp.bfloat16):
    values = jax.random.normal(key, shape, jnp.float32) * width
    if len(pieces) > 0:
        values = block_scale(key, shape, pieces, -0.22, 0.18) * values
    return jnp.clip(values, min=-most, max=most).astype(kind)


def setup_inputs(seed: int = 0) -> dict:
    streams_of = jax.random.split(jax.random.key(seed), 10)
    queries = draw_queries(jax.random.fold_in(streams_of[9], 71), 0)
    keys = draw_keys(jax.random.fold_in(streams_of[9], 71), 0)
    values = normal_values(streams_of[2], (TOKENS, D), 1.0, 6.0, ((0, 32), (1, 16)))
    rates = jnp.clip(jnp.exp(math.log(1.0) - 2.3025851 * jax.random.uniform(streams_of[3], (TOKENS, HEADS), jnp.float32) ** block_scale(streams_of[3], (TOKENS, HEADS), ((0, 32), (1, 16)), -0.2, 0.2)), 0.1, 1.0)
    w_one = normal_values(streams_of[4], (HEADS, HID, HD), HD ** -0.5, 0.375, ((0, 16),))
    w_three = normal_values(streams_of[5], (HEADS, HID, HD), HD ** -0.5, 0.375, ((0, 16),))
    w_two = normal_values(streams_of[6], (HEADS, HD, HID), HID ** -0.5, 0.375, ((0, 16),))
    gain = jnp.clip(1.0 + 0.1 * jax.random.normal(streams_of[7], (D,), jnp.float32), 0.5, 1.5)
    order = draw_order(jax.random.fold_in(streams_of[9], 71), 0)
    return dict(queries=queries, keys=keys, values=values, rates=rates, w_one=w_one, w_three=w_three, w_two=w_two, gain=gain, order=order)


EPSILON = 1e-06

def renew(weight, grad):
    wf = weight.astype(jnp.float32)
    scale = jnp.sqrt(jnp.mean(wf * wf)) / jnp.sqrt(jnp.mean(grad * grad) + EPSILON)
    moved = wf - scale * grad
    ratio = jnp.sqrt(lax.optimization_barrier(jnp.sum(wf * wf, axis=-1, keepdims=True))) / jnp.sqrt(lax.optimization_barrier(jnp.sum(moved * moved, axis=-1, keepdims=True)) + EPSILON)
    return (moved * ratio).astype(jnp.bfloat16)

def reference(queries, keys, values, rates, w_one, w_three, w_two, gain, order):
    inverse = jnp.argsort(order, axis=1).astype(jnp.int32)

    def arrange(data):
        data = data.reshape(CAMERAS, TOK_DEV, HD)
        data = jax.vmap(lambda rows, index: jnp.take(rows, index, axis=0))(data, inverse)
        data = data.reshape(CAMERAS, FRAMES, PATCHES, HD).transpose(1, 0, 2, 3)
        return data.reshape(FRAMES, CAMERAS * PATCHES, HD)

    def restore(data):
        data = data.reshape(FRAMES, CAMERAS, PATCHES, HD).transpose(1, 0, 2, 3).reshape(CAMERAS, TOK_DEV, HD)
        data = jax.vmap(lambda rows, index: jnp.take(rows, index, axis=0))(data, order)
        return data.reshape(TOKENS, HD)

    def attend_frame(block):
        query_rows, key_rows, value_rows = block
        scores = jnp.dot(query_rows, key_rows.T, preferred_element_type=jnp.float32) * HD ** (-0.5)
        scores = scores - lax.optimization_barrier(jnp.max(scores, axis=-1, keepdims=True))
        expo = jnp.exp(scores)
        probs = (expo / lax.optimization_barrier(jnp.sum(expo, axis=-1, keepdims=True))).astype(jnp.bfloat16)
        return jnp.dot(probs, value_rows, preferred_element_type=jnp.float32).astype(jnp.bfloat16)

    def one_head(head):
        start = head * HD
        query = lax.dynamic_slice_in_dim(queries, start, HD, 1)
        key = lax.dynamic_slice_in_dim(keys, start, HD, 1)
        value = lax.dynamic_slice_in_dim(values, start, HD, 1)
        rate = lax.dynamic_slice_in_dim(rates, head, 1, 1)
        first = w_one[head]
        third = w_three[head]
        second = w_two[head]
        h_one = jnp.dot(key, first.T, preferred_element_type=jnp.float32)
        h_three = jnp.dot(key, third.T, preferred_element_type=jnp.float32)
        sigma = jax.nn.sigmoid(h_one)
        active = (h_one * sigma * h_three).astype(jnp.bfloat16)
        error = (-rate * value.astype(jnp.float32)).astype(jnp.bfloat16)
        grad_second = jnp.dot(error.T, active, preferred_element_type=jnp.float32)
        back = jnp.dot(error, second, preferred_element_type=jnp.float32)
        back_one = (back * h_three * sigma * (1.0 + h_one * (1.0 - sigma))).astype(jnp.bfloat16)
        back_three = (back * h_one * sigma).astype(jnp.bfloat16)
        grad_first = jnp.dot(back_one.T, key, preferred_element_type=jnp.float32)
        grad_third = jnp.dot(back_three.T, key, preferred_element_type=jnp.float32)
        new_first = renew(first, grad_first)
        new_third = renew(third, grad_third)
        new_second = renew(second, grad_second)
        q_one = jnp.dot(query, new_first.T, preferred_element_type=jnp.float32)
        q_three = jnp.dot(query, new_third.T, preferred_element_type=jnp.float32)
        q_active = (q_one * jax.nn.sigmoid(q_one) * q_three).astype(jnp.bfloat16)
        readout = jnp.dot(q_active, new_second.T, preferred_element_type=jnp.float32)
        attended = lax.map(attend_frame, (arrange(query), arrange(key), arrange(value)))
        return (readout, restore(attended))
    readouts, attended = lax.map(one_head, jnp.arange(HEADS, dtype=jnp.int32))
    total = lax.optimization_barrier(jnp.sum(readouts * readouts, axis=(0, 2)))
    inv_norm = 1.0 / jnp.sqrt(total / D + EPSILON)
    mixed = readouts * inv_norm[None, :, None] * gain.reshape(HEADS, 1, HD) + attended.astype(jnp.float32)
    return mixed.transpose(1, 0, 2).reshape(TOKENS, D).astype(jnp.bfloat16)
```

```python
import functools
import jax
import jax.numpy as jnp
from jax import lax
from jax.experimental import pallas as pl
from jax.experimental.pallas import tpu as pltpu
from jax.sharding import PartitionSpec as P

PATCHES = 32
EPSILON = 1e-06
GROUP = 8
PLANE = 4
MESH = pl.DeviceIdType.MESH
F32 = jnp.float32
BF16 = jnp.bfloat16


def nt(a, b):
    return lax.dot_general(a, b, (((1,), (1,)), ((), ())), preferred_element_type=F32)


def nn(a, b):
    return jnp.dot(a, b, preferred_element_type=F32)


def column_of(row):
    return jnp.transpose(jnp.broadcast_to(row, (128, 128)))


def drain(ref, sem):
    pltpu.make_async_copy(ref, ref, sem).wait()


def renewed(weight, grad):
    wf = weight.astype(F32)
    scale = jnp.sqrt(jnp.mean(wf * wf)) / jnp.sqrt(jnp.mean(grad * grad) + EPSILON)
    moved = wf - scale * grad
    ratio = jnp.sqrt(jnp.sum(wf * wf, axis=1, keepdims=True)) / jnp.sqrt(
        jnp.sum(moved * moved, axis=1, keepdims=True) + EPSILON
    )
    return (moved * ratio).astype(BF16)


def layer(
    cams, heads,
    q_ref, k_ref, v_ref, rates_ref, w1_ref, w3_ref, w2_ref, gain_ref, order_ref,
    out_ref,
    sbuf, rbuf, obuf, ret, gbuf, gall, plane_in, line_in, line_own, u_buf, y_buf,
    rcol, ocol, sq_own, sq_in,
    bulk_send, bulk_recv, back_send, back_recv,
    g_send, g_recv, sq_send, sq_recv,
):
    count, width = q_ref.shape
    lines = cams // PLANE
    blocks = cams // GROUP
    rows = GROUP * PATCHES
    frame_rows = cams * PATCHES
    hid = w1_ref.shape[0]
    plane_rows = hid // PLANE
    line_rows = plane_rows // lines
    cam = lax.axis_index("cam")
    head = lax.axis_index("head")
    line, place = cam // PLANE, cam % PLANE

    barrier = pltpu.get_barrier_semaphore()

    def greet_cam(o, c):
        pl.semaphore_signal(
            barrier, inc=1, device_id=((cam + o) % cams, head), device_id_type=MESH
        )
        return c

    def greet_head(o, c):
        pl.semaphore_signal(
            barrier, inc=1, device_id=(cam, (head + o) % heads), device_id_type=MESH
        )
        return c

    lax.fori_loop(1, cams, greet_cam, 0)
    lax.fori_loop(1, heads, greet_head, 0)

    def block_at(turn):
        return (cam // GROUP + turn) % blocks

    def sort_block(frame, turn):
        blk = block_at(turn)
        first = frame * frame_rows + blk * rows
        slot = lax.broadcasted_iota(jnp.int32, (rows, count), 0) + first
        pick = jnp.where(slot == order_ref[...], 1.0, 0.0).astype(BF16)
        for a, ref in enumerate((q_ref, k_ref, v_ref)):
            got = nn(pick, ref[...]).astype(BF16).reshape(GROUP, PATCHES, width)
            sbuf[frame, pl.ds(blk * GROUP, GROUP), a] = got

    def send_block(frame, turn):
        blk = block_at(turn)

        def one(j, c):
            dest = blk * GROUP + (cam + j) % GROUP
            pltpu.make_async_remote_copy(
                src_ref=sbuf.at[frame, dest],
                dst_ref=rbuf.at[frame, cam],
                send_sem=bulk_send.at[frame],
                recv_sem=bulk_recv.at[frame],
                device_id=(dest, head),
                device_id_type=MESH,
            ).start()
            return c

        if turn == 0:
            pltpu.make_async_copy(
                sbuf.at[frame, cam], rbuf.at[frame, cam], bulk_recv.at[frame]
            ).start()
        lax.fori_loop(1 if turn == 0 else 0, GROUP, one, 0)

    def attend_block(frame, turn):
        blk = block_at(turn)
        query = rbuf[frame, pl.ds(blk * GROUP, GROUP), 0].reshape(rows, width)
        key = rbuf[frame, :, 1].reshape(frame_rows, width)
        value = rbuf[frame, :, 2].reshape(frame_rows, width)
        scores = nt(query, key) * (width ** (-0.5))
        expo = jnp.exp(scores - jnp.max(scores, axis=1, keepdims=True))
        probs = (expo * (1.0 / jnp.sum(expo, axis=1, keepdims=True))).astype(BF16)
        got = nn(probs, value).astype(BF16).reshape(GROUP, PATCHES, width)
        obuf[frame, pl.ds(blk * GROUP, GROUP)] = got

    def return_block(frame, turn):
        blk = block_at(turn)

        def one(j, c):
            dest = blk * GROUP + (cam + j) % GROUP
            pltpu.make_async_remote_copy(
                src_ref=obuf.at[frame, dest],
                dst_ref=ret.at[frame, cam],
                send_sem=back_send.at[frame],
                recv_sem=back_recv.at[frame],
                device_id=(dest, head),
                device_id_type=MESH,
            ).start()
            return c

        if turn == 0:
            pltpu.make_async_copy(
                obuf.at[frame, cam], ret.at[frame, cam], back_recv.at[frame]
            ).start()
        lax.fori_loop(1 if turn == 0 else 0, GROUP, one, 0)

    turns = [t for t in (2, 1, 3, 0) if t < blocks]
    early, late = turns[: blocks // 2], turns[blocks // 2 :]

    def columns(b, c):
        lanes = pl.ds(pl.multiple_of(b * 128, 128), 128)
        here = pl.ds(pl.multiple_of(b * 128, 128), 128)
        rcol[here] = column_of(rates_ref[:, lanes])
        ocol[here] = column_of(order_ref[:, lanes].astype(F32))
        return c

    def grad_step(i, c):
        step = 512
        here = pl.ds(pl.multiple_of(i * step, step), step)
        key, val = k_ref[here], v_ref[here].astype(F32)
        rate = rcol[here]
        err = (-jnp.concatenate([rate, rate], axis=1) * val).astype(BF16)
        a1, a3 = nt(w1_ref[...], key), nt(w3_ref[...], key)
        s = jax.nn.sigmoid(a1)
        act = (a1 * s * a3).astype(BF16)
        back = nt(u_buf[0], err)
        b1 = (back * a3 * s * (1.0 + a1 * (1.0 - s))).astype(BF16)
        b3 = (back * a1 * s).astype(BF16)
        gbuf[0] += nn(b1, key)
        gbuf[1] += nn(b3, key)
        gbuf[2] += nn(act, err)
        return c

    def plane_peer(o):
        return (line * PLANE + (place + o) % PLANE, head)

    def line_peer(o):
        return (((line + o) % lines) * PLANE + place, head)

    def stage(n, src, dst, peer):
        pltpu.make_async_remote_copy(
            src_ref=src, dst_ref=dst, send_sem=g_send.at[n], recv_sem=g_recv.at[n],
            device_id=peer, device_id_type=MESH,
        ).start()

    sort_block(0, early[0] if early else turns[0])
    pl.semaphore_wait(barrier, cams - 1 + heads - 1)
    send_block(0, early[0] if early else turns[0])
    for t in early[1:]:
        sort_block(0, t)
        send_block(0, t)

    lax.fori_loop(0, count // 128, columns, 0)
    u_buf[0] = jnp.transpose(w2_ref[...].astype(F32)).astype(BF16)
    gbuf[...] = jnp.zeros_like(gbuf)
    lax.fori_loop(0, count // 512, grad_step, 0)
    for o in range(1, PLANE):
        theirs = pl.ds(((place + o) % PLANE) * plane_rows, plane_rows)
        stage(0, gbuf.at[:, theirs], plane_in.at[o - 1], plane_peer(o))
    for t in (late if early else late[1:]):
        sort_block(0, t)
        send_block(0, t)
    drain(plane_in, g_recv.at[0])
    drain(plane_in, g_send.at[0])
    mine = pl.ds(place * plane_rows, plane_rows)
    gbuf[:, mine] += plane_in[0] + plane_in[1] + plane_in[2]

    sort_block(1, turns[0])
    for o in range(1, lines):
        theirs = pl.ds(place * plane_rows + ((line + o) % lines) * line_rows, line_rows)
        stage(1, gbuf.at[:, theirs], line_in.at[o - 1], line_peer(o))
    send_block(1, turns[0])
    for t in turns[1:2]:
        sort_block(1, t)
        send_block(1, t)
    drain(line_in, g_recv.at[1])
    drain(line_in, g_send.at[1])
    own = pl.ds(place * plane_rows + line * line_rows, line_rows)
    total = gbuf[:, own]
    for o in range(1, lines):
        total = total + line_in[o - 1]
    line_own[...] = total
    gall[:, own] = total
    for t in turns[2:3]:
        sort_block(1, t)
    for o in range(1, lines):
        stage(2, line_own, gall.at[:, own], line_peer(o))
    for t in turns[2:3]:
        send_block(1, t)
    for t in turns[3:]:
        sort_block(1, t)
    drain(line_in, g_recv.at[2])
    drain(line_in, g_send.at[2])
    for o in range(1, PLANE):
        stage(3, gall.at[:, mine], gall.at[:, mine], plane_peer(o))
    for t in turns[3:]:
        send_block(1, t)
    drain(plane_in, g_recv.at[3])
    drain(plane_in, g_send.at[3])

    u_buf[0] = renewed(w1_ref[...], gall[0])
    u_buf[1] = renewed(w3_ref[...], gall[1])
    u_buf[2] = renewed(w2_ref[...], jnp.transpose(gall[2]))

    def readout(i, c):
        step = 256
        here = pl.ds(pl.multiple_of(i * step, step), step)
        query = q_ref[here]
        q1, q3 = nt(query, u_buf[0]), nt(query, u_buf[1])
        act = (q1 * jax.nn.sigmoid(q1) * q3).astype(BF16)
        y = nt(act, u_buf[2])
        y_buf[here] = y
        half = y[:, :128] * y[:, :128] + y[:, 128:] * y[:, 128:]
        for b in range(step // 128):
            part = jnp.sum(jnp.transpose(half[b * 128 : (b + 1) * 128]), axis=0, keepdims=True)
            sq_own[pl.ds(i * (step // 128) + b, 1)] = part
        return c

    lax.fori_loop(0, count // 256, readout, 0)

    def send_sq(o, c):
        pltpu.make_async_remote_copy(
            src_ref=sq_own, dst_ref=sq_in.at[o - 1], send_sem=sq_send, recv_sem=sq_recv,
            device_id=(cam, (head + o) % heads), device_id_type=MESH,
        ).start()
        return c

    drain(rbuf.at[0], bulk_recv.at[0])
    attend_block(0, turns[0])
    lax.fori_loop(1, heads, send_sq, 0)
    for a, b in zip(turns[1:], turns[:-1]):
        attend_block(0, a)
        return_block(0, b)
    drain(rbuf.at[1], bulk_recv.at[1])
    attend_block(1, turns[0])
    return_block(0, turns[-1])
    for a, b in zip(turns[1:], turns[:-1]):
        attend_block(1, a)
        return_block(1, b)

    drain(sq_in, sq_recv)
    square = sq_own[...]
    for o in range(1, heads):
        square = square + sq_in[o - 1]
    sq_own_inv = 1.0 / jnp.sqrt(square / (width * heads) + EPSILON)
    drain(sq_in, sq_send)
    return_block(1, turns[-1])
    sq_own[...] = sq_own_inv

    def scaled(b, c):
        here = pl.ds(pl.multiple_of(b * 128, 128), 128)
        inv = column_of(sq_own[pl.ds(b, 1)])
        y_buf[here] = y_buf[here] * jnp.concatenate([inv, inv], axis=1) * gain_ref[...]
        return c

    lax.fori_loop(0, count // 128, scaled, 0)

    def taken(frame, here, step):
        at = ocol[here]
        lane = lax.broadcasted_iota(jnp.int32, (step, 128), 1).astype(F32)
        pick = jnp.concatenate(
            [
                jnp.where(at == lane + float(frame * frame_rows + b * 128), 1.0, 0.0).astype(BF16)
                for b in range(frame_rows // 128)
            ],
            axis=1,
        )
        return nn(pick, ret[frame].reshape(frame_rows, width))

    drain(ret.at[0], back_recv.at[0])

    def first_half(i, c):
        here = pl.ds(pl.multiple_of(i * 256, 256), 256)
        y_buf[here] += taken(0, here, 256)
        return c

    lax.fori_loop(0, count // 256, first_half, 0)
    drain(ret.at[1], back_recv.at[1])

    def second_half(i, c):
        here = pl.ds(pl.multiple_of(i * 256, 256), 256)
        out_ref[here] = (y_buf[here] + taken(1, here, 256)).astype(BF16)
        return c

    lax.fori_loop(0, count // 256, second_half, 0)
    for frame in range(2):
        drain(sbuf.at[frame, pl.ds(0, cams - 1)], bulk_send.at[frame])
        drain(obuf.at[frame, pl.ds(0, cams - 1)], back_send.at[frame])


def per_device(cams, heads, queries, keys, values, rates, w_one, w_three, w_two, gain, order):
    count, width = queries.shape
    hid = w_one.shape[1]
    plane_rows = hid // PLANE
    lines = cams // PLANE
    line_rows = plane_rows // lines
    dma = pltpu.SemaphoreType.DMA
    vmem = pl.BlockSpec(memory_space=pltpu.VMEM)
    return pl.pallas_call(
        functools.partial(layer, cams, heads),
        out_shape=jax.ShapeDtypeStruct((count, width), BF16),
        in_specs=[vmem] * 9,
        out_specs=vmem,
        scratch_shapes=[
            pltpu.VMEM((2, cams, 3, PATCHES, width), BF16),
            pltpu.VMEM((2, cams, 3, PATCHES, width), BF16),
            pltpu.VMEM((2, cams, PATCHES, width), BF16),
            pltpu.VMEM((2, cams, PATCHES, width), BF16),
            pltpu.VMEM((3, hid, width), F32),
            pltpu.VMEM((3, hid, width), F32),
            pltpu.VMEM((PLANE - 1, 3, plane_rows, width), F32),
            pltpu.VMEM((lines - 1, 3, line_rows, width), F32),
            pltpu.VMEM((3, line_rows, width), F32),
            pltpu.VMEM((3, hid, width), BF16),
            pltpu.VMEM((count, width), F32),
            pltpu.VMEM((count, 128), F32),
            pltpu.VMEM((count, 128), F32),
            pltpu.VMEM((count // 128, 128), F32),
            pltpu.VMEM((heads - 1, count // 128, 128), F32),
            dma((2,)),
            dma((2,)),
            dma((2,)),
            dma((2,)),
            dma((4,)),
            dma((4,)),
            dma,
            dma,
        ],
        compiler_params=pltpu.CompilerParams(
            collective_id=0, has_side_effects=True, vmem_limit_bytes=60 * 1024 * 1024
        ),
        name="layer",
    )(
        queries, keys, values, rates.reshape(1, count),
        w_one[0], w_three[0], w_two[0], gain.reshape(1, width), order,
    )


def solution(mesh):
    in_specs = (
        P("cam", "head"),
        P("cam", "head"),
        P("cam", "head"),
        P("cam", "head"),
        P("head", None, None),
        P("head", None, None),
        P("head", None, None),
        P("head"),
        P("cam", None),
    )
    step = functools.partial(per_device, mesh.shape["cam"], mesh.shape["head"])
    return jax.shard_map(
        step, mesh=mesh, in_specs=in_specs, out_specs=P("cam", "head"), check_vma=False
    )
```

```python
import functools
import jax
import jax.numpy as jnp
from jax import lax
from jax.experimental import pallas as pl
from jax.experimental.pallas import tpu as pltpu
from jax.sharding import PartitionSpec as P

PATCHES = 32
EPSILON = 1e-06
GROUP = 8
PLANE = 4
MESH = pl.DeviceIdType.MESH
F32 = jnp.float32
BF16 = jnp.bfloat16


def nt(a, b):
    return lax.dot_general(a, b, (((1,), (1,)), ((), ())), preferred_element_type=F32)


def nn(a, b):
    return jnp.dot(a, b, preferred_element_type=F32)


def column_of(row):
    return jnp.transpose(jnp.broadcast_to(row, (128, 128)))


def drain(ref, sem):
    pltpu.make_async_copy(ref, ref, sem).wait()


def renewed(weight, grad):
    wf = weight.astype(F32)
    scale = jnp.sqrt(jnp.mean(wf * wf)) / jnp.sqrt(jnp.mean(grad * grad) + EPSILON)
    moved = wf - scale * grad
    ratio = jnp.sqrt(jnp.sum(wf * wf, axis=1, keepdims=True)) / jnp.sqrt(
        jnp.sum(moved * moved, axis=1, keepdims=True) + EPSILON
    )
    return (moved * ratio).astype(BF16)


def layer(
    cams, heads,
    q_ref, k_ref, v_ref, rates_ref, w1_ref, w3_ref, w2_ref, gain_ref, order_ref,
    out_ref,
    sbuf, rbuf, obuf, ret, gbuf, gall, plane_in, line_in, u_buf, y_buf,
    rcol, ocol, sq_own, sq_in,
    bulk_send, bulk_recv, back_send, back_recv,
    g_send, g_recv, sq_send, sq_recv,
):
    count, width = q_ref.shape
    lines = cams // PLANE
    blocks = cams // GROUP
    rows = GROUP * PATCHES
    frame_rows = cams * PATCHES
    hid = w1_ref.shape[0]
    plane_rows = hid // PLANE
    line_rows = plane_rows // lines
    cam = lax.axis_index("cam")
    head = lax.axis_index("head")
    line, place = cam // PLANE, cam % PLANE

    barrier = pltpu.get_barrier_semaphore()

    def greet_cam(o, c):
        pl.semaphore_signal(
            barrier, inc=1, device_id=((cam + o) % cams, head), device_id_type=MESH
        )
        return c

    def greet_head(o, c):
        pl.semaphore_signal(
            barrier, inc=1, device_id=(cam, (head + o) % heads), device_id_type=MESH
        )
        return c

    lax.fori_loop(1, cams, greet_cam, 0)
    lax.fori_loop(1, heads, greet_head, 0)

    def block_at(turn):
        return (cam // GROUP + turn) % blocks

    def sort_block(frame, turn):
        blk = block_at(turn)
        first = frame * frame_rows + blk * rows
        slot = lax.broadcasted_iota(jnp.int32, (rows, count), 0) + first
        pick = jnp.where(slot == order_ref[...], 1.0, 0.0).astype(BF16)
        for a, ref in enumerate((q_ref, k_ref, v_ref)):
            got = nn(pick, ref[...]).astype(BF16).reshape(GROUP, PATCHES, width)
            sbuf[frame, pl.ds(blk * GROUP, GROUP), a] = got

    def send_block(frame, turn):
        blk = block_at(turn)

        def one(j, c):
            dest = blk * GROUP + (cam + j) % GROUP
            pltpu.make_async_remote_copy(
                src_ref=sbuf.at[frame, dest],
                dst_ref=rbuf.at[frame, cam],
                send_sem=bulk_send.at[frame],
                recv_sem=bulk_recv.at[frame],
                device_id=(dest, head),
                device_id_type=MESH,
            ).start()
            return c

        if turn == 0:
            pltpu.make_async_copy(
                sbuf.at[frame, cam], rbuf.at[frame, cam], bulk_recv.at[frame]
            ).start()
        lax.fori_loop(1 if turn == 0 else 0, GROUP, one, 0)

    def attend_block(frame, turn):
        blk = block_at(turn)
        query = rbuf[frame, pl.ds(blk * GROUP, GROUP), 0].reshape(rows, width)
        key = rbuf[frame, :, 1].reshape(frame_rows, width)
        value = rbuf[frame, :, 2].reshape(frame_rows, width)
        scores = nt(query, key) * (width ** (-0.5))
        expo = jnp.exp(scores - jnp.max(scores, axis=1, keepdims=True))
        probs = (expo * (1.0 / jnp.sum(expo, axis=1, keepdims=True))).astype(BF16)
        got = nn(probs, value).astype(BF16).reshape(GROUP, PATCHES, width)
        obuf[frame, pl.ds(blk * GROUP, GROUP)] = got

    def return_block(frame, turn):
        blk = block_at(turn)

        def one(j, c):
            dest = blk * GROUP + (cam + j) % GROUP
            pltpu.make_async_remote_copy(
                src_ref=obuf.at[frame, dest],
                dst_ref=ret.at[frame, cam],
                send_sem=back_send.at[frame],
                recv_sem=back_recv.at[frame, turn],
                device_id=(dest, head),
                device_id_type=MESH,
            ).start()
            return c

        if turn == 0:
            pltpu.make_async_copy(
                obuf.at[frame, cam], ret.at[frame, cam], back_recv.at[frame, turn]
            ).start()
        lax.fori_loop(1 if turn == 0 else 0, GROUP, one, 0)

    turns = [t for t in (2, 1, 3, 0) if t < blocks]

    def columns(b, c):
        lanes = pl.ds(pl.multiple_of(b * 128, 128), 128)
        here = pl.ds(pl.multiple_of(b * 128, 128), 128)
        rcol[here] = column_of(rates_ref[:, lanes])
        ocol[here] = column_of(order_ref[:, lanes].astype(F32))
        return c

    def grad_step(i, c):
        step = 512
        here = pl.ds(pl.multiple_of(i * step, step), step)
        key, val = k_ref[here], v_ref[here].astype(F32)
        rate = rcol[here]
        err = (-jnp.concatenate([rate, rate], axis=1) * val).astype(BF16)
        a1, a3 = nt(w1_ref[...], key), nt(w3_ref[...], key)
        s = jax.nn.sigmoid(a1)
        act = (a1 * s * a3).astype(BF16)
        back = nt(u_buf[0], err)
        b1 = (back * a3 * s * (1.0 + a1 * (1.0 - s))).astype(BF16)
        b3 = (back * a1 * s).astype(BF16)
        gbuf[0] += nn(b1, key)
        gbuf[1] += nn(b3, key)
        gbuf[2] += nn(act, err)
        return c

    def plane_peer(o):
        return (line * PLANE + (place + o) % PLANE, head)

    def line_peer(o):
        return (((line + o) % lines) * PLANE + place, head)

    def stage(n, src, dst, peer):
        pltpu.make_async_remote_copy(
            src_ref=src, dst_ref=dst, send_sem=g_send.at[n], recv_sem=g_recv.at[n],
            device_id=peer, device_id_type=MESH,
        ).start()

    lax.fori_loop(0, count // 128, columns, 0)
    u_buf[0] = jnp.transpose(w2_ref[...].astype(F32)).astype(BF16)
    gbuf[...] = jnp.zeros_like(gbuf)
    lax.fori_loop(0, count // 512, grad_step, 0)
    sort_block(0, turns[0])
    pl.semaphore_wait(barrier, cams - 1 + heads - 1)

    for o in range(1, PLANE):
        theirs = pl.ds(((place + o) % PLANE) * plane_rows, plane_rows)
        stage(0, gbuf.at[:, theirs], plane_in.at[o - 1], plane_peer(o))
    send_block(0, turns[0])
    for t in turns[1:2]:
        sort_block(0, t)
        send_block(0, t)
    drain(plane_in, g_recv.at[0])
    drain(plane_in, g_send.at[0])
    mine = pl.ds(place * plane_rows, plane_rows)
    gbuf[:, mine] += plane_in[0] + plane_in[1] + plane_in[2]

    for t in turns[2:3]:
        sort_block(0, t)
    for o in range(1, lines):
        theirs = pl.ds(place * plane_rows + ((line + o) % lines) * line_rows, line_rows)
        stage(1, gbuf.at[:, theirs], line_in.at[o - 1], line_peer(o))
    for t in turns[2:3]:
        send_block(0, t)
    for t in turns[3:]:
        sort_block(0, t)
        send_block(0, t)
    drain(line_in, g_recv.at[1])
    drain(line_in, g_send.at[1])
    own = pl.ds(place * plane_rows + line * line_rows, line_rows)
    total = gbuf[:, own]
    for o in range(1, lines):
        total = total + line_in[o - 1]
    gall[:, own] = total
    sort_block(1, turns[0])

    for o in range(1, lines):
        stage(2, gall.at[:, own], gall.at[:, own], line_peer(o))
    send_block(1, turns[0])
    for t in turns[1:2]:
        sort_block(1, t)
        send_block(1, t)
    drain(line_in, g_recv.at[2])
    drain(line_in, g_send.at[2])
    for o in range(1, PLANE):
        stage(3, gall.at[:, mine], gall.at[:, mine], plane_peer(o))
    for t in turns[2:]:
        sort_block(1, t)
        send_block(1, t)

    drain(rbuf.at[0], bulk_recv.at[0])
    attend_block(0, turns[0])
    for a, b in zip(turns[1:], turns[:-1]):
        attend_block(0, a)
        return_block(0, b)
    return_block(0, turns[-1])
    drain(plane_in, g_recv.at[3])
    drain(plane_in, g_send.at[3])

    u_buf[0] = renewed(w1_ref[...], gall[0])
    u_buf[1] = renewed(w3_ref[...], gall[1])
    u_buf[2] = renewed(w2_ref[...], jnp.transpose(gall[2]))

    def readout(i, c):
        step = 256
        here = pl.ds(pl.multiple_of(i * step, step), step)
        query = q_ref[here]
        q1, q3 = nt(query, u_buf[0]), nt(query, u_buf[1])
        act = (q1 * jax.nn.sigmoid(q1) * q3).astype(BF16)
        y = nt(act, u_buf[2])
        y_buf[here] = y
        half = y[:, :128] * y[:, :128] + y[:, 128:] * y[:, 128:]
        for b in range(step // 128):
            part = jnp.sum(jnp.transpose(half[b * 128 : (b + 1) * 128]), axis=0, keepdims=True)
            sq_own[pl.ds(i * (step // 128) + b, 1)] = part
        return c

    lax.fori_loop(0, count // 256, readout, 0)

    def send_sq(o, c):
        pltpu.make_async_remote_copy(
            src_ref=sq_own, dst_ref=sq_in.at[o - 1], send_sem=sq_send, recv_sem=sq_recv,
            device_id=(cam, (head + o) % heads), device_id_type=MESH,
        ).start()
        return c

    drain(rbuf.at[1], bulk_recv.at[1])
    attend_block(1, turns[0])
    lax.fori_loop(1, heads, send_sq, 0)
    for a, b in zip(turns[1:], turns[:-1]):
        attend_block(1, a)
        return_block(1, b)

    drain(sq_in, sq_send)
    return_block(1, turns[-1])
    drain(sq_in, sq_recv)
    square = sq_own[...]
    for o in range(1, heads):
        square = square + sq_in[o - 1]
    sq_own_inv = 1.0 / jnp.sqrt(square / (width * heads) + EPSILON)
    sq_own[...] = sq_own_inv

    def scaled(b, c):
        here = pl.ds(pl.multiple_of(b * 128, 128), 128)
        inv = column_of(sq_own[pl.ds(b, 1)])
        y_buf[here] = y_buf[here] * jnp.concatenate([inv, inv], axis=1) * gain_ref[...]
        return c

    lax.fori_loop(0, count // 128, scaled, 0)

    def take(frame, turn, last):
        owners = pl.ds(((cam // GROUP - turn) % blocks) * GROUP, GROUP)
        first = (frame * frame_rows + ((cam // GROUP - turn) % blocks) * rows).astype(F32)
        drain(ret.at[frame, owners], back_recv.at[frame, turn])

        def step(i, c):
            here = pl.ds(pl.multiple_of(i * 256, 256), 256)
            at = ocol[here] - first
            lane = lax.broadcasted_iota(jnp.int32, (256, 128), 1).astype(F32)
            pick = jnp.concatenate(
                [jnp.where(at == lane + float(b), 1.0, 0.0).astype(BF16) for b in range(0, rows, 128)],
                axis=1,
            )
            got = y_buf[here] + nn(pick, ret[frame, owners].reshape(rows, width))
            if last:
                out_ref[here] = got.astype(BF16)
            else:
                y_buf[here] = got
            return c

        lax.fori_loop(0, count // 256, step, 0)

    for frame in range(2):
        for t in turns:
            take(frame, t, frame == 1 and t == turns[-1])
    for frame in range(2):
        drain(sbuf.at[frame, pl.ds(0, cams - 1)], bulk_send.at[frame])
        drain(obuf.at[frame, pl.ds(0, cams - 1)], back_send.at[frame])


def per_device(cams, heads, queries, keys, values, rates, w_one, w_three, w_two, gain, order):
    count, width = queries.shape
    hid = w_one.shape[1]
    plane_rows = hid // PLANE
    lines = cams // PLANE
    line_rows = plane_rows // lines
    dma = pltpu.SemaphoreType.DMA
    vmem = pl.BlockSpec(memory_space=pltpu.VMEM)
    return pl.pallas_call(
        functools.partial(layer, cams, heads),
        out_shape=jax.ShapeDtypeStruct((count, width), BF16),
        in_specs=[vmem] * 9,
        out_specs=vmem,
        scratch_shapes=[
            pltpu.VMEM((2, cams, 3, PATCHES, width), BF16),
            pltpu.VMEM((2, cams, 3, PATCHES, width), BF16),
            pltpu.VMEM((2, cams, PATCHES, width), BF16),
            pltpu.VMEM((2, cams, PATCHES, width), BF16),
            pltpu.VMEM((3, hid, width), F32),
            pltpu.VMEM((3, hid, width), F32),
            pltpu.VMEM((PLANE - 1, 3, plane_rows, width), F32),
            pltpu.VMEM((lines - 1, 3, line_rows, width), F32),
            pltpu.VMEM((3, hid, width), BF16),
            pltpu.VMEM((count, width), F32),
            pltpu.VMEM((count, 128), F32),
            pltpu.VMEM((count, 128), F32),
            pltpu.VMEM((count // 128, 128), F32),
            pltpu.VMEM((heads - 1, count // 128, 128), F32),
            dma((2,)),
            dma((2,)),
            dma((2,)),
            dma((2, cams // GROUP)),
            dma((4,)),
            dma((4,)),
            dma,
            dma,
        ],
        compiler_params=pltpu.CompilerParams(
            collective_id=0, has_side_effects=True, vmem_limit_bytes=60 * 1024 * 1024
        ),
        name="layer",
    )(
        queries, keys, values, rates.reshape(1, count),
        w_one[0], w_three[0], w_two[0], gain.reshape(1, width), order,
    )


def solution(mesh):
    in_specs = (
        P("cam", "head"),
        P("cam", "head"),
        P("cam", "head"),
        P("cam", "head"),
        P("head", None, None),
        P("head", None, None),
        P("head", None, None),
        P("head"),
        P("cam", None),
    )
    step = functools.partial(per_device, mesh.shape["cam"], mesh.shape["head"])
    return jax.shard_map(
        step, mesh=mesh, in_specs=in_specs, out_specs=P("cam", "head"), check_vma=False
    )
```

```python
import functools
import jax
import jax.numpy as jnp
from jax import lax
from jax.experimental import pallas as pl
from jax.experimental.pallas import tpu as pltpu
from jax.sharding import PartitionSpec as P

PATCHES = 32
EPSILON = 1e-06
GROUP = 8
PLANE = 4
MESH = pl.DeviceIdType.MESH
F32 = jnp.float32
BF16 = jnp.bfloat16


def nt(a, b):
    return lax.dot_general(a, b, (((1,), (1,)), ((), ())), preferred_element_type=F32)


def nn(a, b):
    return jnp.dot(a, b, preferred_element_type=F32)


def column_of(row):
    return jnp.transpose(jnp.broadcast_to(row, (128, 128)))


def drain(ref, sem):
    pltpu.make_async_copy(ref, ref, sem).wait()


def renewed(weight, grad):
    wf = weight.astype(F32)
    scale = jnp.sqrt(jnp.mean(wf * wf)) / jnp.sqrt(jnp.mean(grad * grad) + EPSILON)
    moved = wf - scale * grad
    ratio = jnp.sqrt(jnp.sum(wf * wf, axis=1, keepdims=True)) / jnp.sqrt(
        jnp.sum(moved * moved, axis=1, keepdims=True) + EPSILON
    )
    return (moved * ratio).astype(BF16)


def layer(
    cams, heads,
    q_hbm, k_hbm, v_hbm, rates_hbm, w1_hbm, w3_hbm, w2_hbm, gain_hbm, order_hbm,
    out_hbm,
    q_ref, k_ref, v_ref, rates_ref, w1_ref, w3_ref, w2_ref, gain_ref, order_ref, out_ref,
    acc, pick_b, sbuf, rbuf, obuf, ret, gbuf, gall, plane_in, line_in, u_buf, y_buf,
    rcol, ocol, sq_own, sq_in,
    bulk_send, bulk_recv, back_send, back_recv,
    g_send, g_recv, sq_send, sq_recv, in_sem, out_sem,
):
    count, width = q_ref.shape
    lines = cams // PLANE
    blocks = cams // GROUP
    rows = GROUP * PATCHES
    frame_rows = cams * PATCHES
    hid = w1_ref.shape[0]
    plane_rows = hid // PLANE
    line_rows = plane_rows // lines
    cam = lax.axis_index("cam")
    head = lax.axis_index("head")
    line, place = cam // PLANE, cam % PLANE

    barrier = pltpu.get_barrier_semaphore()

    def greet_cam(o, c):
        pl.semaphore_signal(
            barrier, inc=1, device_id=((cam + o) % cams, head), device_id_type=MESH
        )
        return c

    def greet_head(o, c):
        pl.semaphore_signal(
            barrier, inc=1, device_id=(cam, (head + o) % heads), device_id_type=MESH
        )
        return c

    lax.fori_loop(1, cams, greet_cam, 0)
    lax.fori_loop(1, heads, greet_head, 0)

    def load(n, src, dst):
        copy = pltpu.make_async_copy(src, dst, in_sem.at[n])
        copy.start()
        return copy

    early = [
        load(n, src, dst)
        for n, (src, dst) in enumerate(
            ((order_hbm, order_ref), (q_hbm, q_ref), (k_hbm, k_ref), (v_hbm, v_ref))
        )
    ]
    later = [
        load(n + 4, src, dst)
        for n, (src, dst) in enumerate(
            (
                (rates_hbm, rates_ref), (w1_hbm, w1_ref), (w3_hbm, w3_ref),
                (w2_hbm, w2_ref), (gain_hbm, gain_ref),
            )
        )
    ]

    def block_at(turn):
        return (cam // GROUP + turn) % blocks

    def sort_block(frame, turn):
        blk = block_at(turn)
        first = frame * frame_rows + blk * rows
        slot = lax.broadcasted_iota(jnp.int32, (rows, count), 0) + first
        pick = jnp.where(slot == order_ref[...], 1.0, 0.0).astype(BF16)
        for a, ref in enumerate((q_ref, k_ref, v_ref)):
            got = nn(pick, ref[...]).astype(BF16).reshape(GROUP, PATCHES, width)
            sbuf[frame, pl.ds(blk * GROUP, GROUP), a] = got

    def send_block(frame, turn, half=None):
        blk = block_at(turn)
        low = 1 if turn == 0 else 0
        low, high = {None: (low, GROUP), 0: (low, GROUP // 2), 1: (GROUP // 2, GROUP)}[half]

        def one(j, c):
            dest = blk * GROUP + (cam + j) % GROUP
            pltpu.make_async_remote_copy(
                src_ref=sbuf.at[frame, dest],
                dst_ref=rbuf.at[frame, cam],
                send_sem=bulk_send.at[frame],
                recv_sem=bulk_recv.at[frame],
                device_id=(dest, head),
                device_id_type=MESH,
            ).start()
            return c

        if turn == 0 and half != 1:
            pltpu.make_async_copy(
                sbuf.at[frame, cam], rbuf.at[frame, cam], bulk_recv.at[frame]
            ).start()
        lax.fori_loop(low, high, one, 0)

    def attend_block(frame, turn):
        blk = block_at(turn)
        query = rbuf[frame, pl.ds(blk * GROUP, GROUP), 0].reshape(rows, width)
        key = rbuf[frame, :, 1].reshape(frame_rows, width)
        value = rbuf[frame, :, 2].reshape(frame_rows, width)
        scores = nt(query, key) * (width ** (-0.5))
        expo = jnp.exp(scores - jnp.max(scores, axis=1, keepdims=True))
        probs = (expo * (1.0 / jnp.sum(expo, axis=1, keepdims=True))).astype(BF16)
        got = nn(probs, value).astype(BF16).reshape(GROUP, PATCHES, width)
        obuf[frame, pl.ds(blk * GROUP, GROUP)] = got

    def return_block(frame, turn):
        blk = block_at(turn)

        def one(j, c):
            dest = blk * GROUP + (cam + j) % GROUP
            pltpu.make_async_remote_copy(
                src_ref=obuf.at[frame, dest],
                dst_ref=ret.at[frame, cam],
                send_sem=back_send.at[frame],
                recv_sem=back_recv.at[frame],
                device_id=(dest, head),
                device_id_type=MESH,
            ).start()
            return c

        if turn == 0:
            pltpu.make_async_copy(
                obuf.at[frame, cam], ret.at[frame, cam], back_recv.at[frame]
            ).start()
        lax.fori_loop(1 if turn == 0 else 0, GROUP, one, 0)

    turns = [t for t in (2, 1, 3, 0) if t < blocks]

    def columns(b, c):
        lanes = pl.ds(pl.multiple_of(b * 128, 128), 128)
        here = pl.ds(pl.multiple_of(b * 128, 128), 128)
        rcol[here] = column_of(rates_ref[:, lanes])
        ocol[here] = column_of(order_ref[:, lanes].astype(F32))
        return c

    def grad_step(i, c):
        step = 512
        here = pl.ds(pl.multiple_of(i * step, step), step)
        key, val = k_ref[here], v_ref[here].astype(F32)
        rate = rcol[here]
        err = (-jnp.concatenate([rate, rate], axis=1) * val).astype(BF16)
        a1, a3 = nt(w1_ref[...], key), nt(w3_ref[...], key)
        s = jax.nn.sigmoid(a1)
        act = (a1 * s * a3).astype(BF16)
        back = nt(u_buf[0], err)
        b1 = (back * a3 * s * (1.0 + a1 * (1.0 - s))).astype(BF16)
        b3 = (back * a1 * s).astype(BF16)
        gbuf[0] += nn(b1, key)
        gbuf[1] += nn(b3, key)
        gbuf[2] += nn(act, err)
        return c

    def pick_of(frame, here, step):
        at = ocol[here]
        lane = lax.broadcasted_iota(jnp.int32, (step, 128), 1).astype(F32)
        return jnp.concatenate(
            [
                jnp.where(at == lane + float(frame * frame_rows + b), 1.0, 0.0).astype(BF16)
                for b in range(0, frame_rows, 128)
            ],
            axis=1,
        )

    def build_pick(i, c):
        here = pl.ds(pl.multiple_of(i * 256, 256), 256)
        pick_b[here] = pick_of(1, here, 256)
        return c

    def plane_peer(o):
        return (line * PLANE + (place + o) % PLANE, head)

    def line_peer(o):
        return (((line + o) % lines) * PLANE + place, head)

    def stage(n, src, dst, peer):
        pltpu.make_async_remote_copy(
            src_ref=src, dst_ref=dst, send_sem=g_send.at[n], recv_sem=g_recv.at[n],
            device_id=peer, device_id_type=MESH,
        ).start()

    far, sides, near = turns[:1], turns[1:-1], turns[-1:]
    if len(turns) == 1:
        far, near = turns, []

    for copy in early:
        copy.wait()
    for t in far:
        sort_block(0, t)
    pl.semaphore_wait(barrier, cams - 1 + heads - 1)
    for t in far:
        send_block(0, t)

    for copy in later:
        copy.wait()
    lax.fori_loop(0, count // 128, columns, 0)
    u_buf[0] = jnp.transpose(w2_ref[...].astype(F32)).astype(BF16)
    gbuf[...] = jnp.zeros_like(gbuf)
    lax.fori_loop(0, count // 512, grad_step, 0)
    for t in sides[:1]:
        sort_block(0, t)
    for o in range(1, PLANE):
        theirs = pl.ds(((place + o) % PLANE) * plane_rows, plane_rows)
        stage(0, gbuf.at[:, theirs], plane_in.at[o - 1], plane_peer(o))
    for t in sides[1:]:
        sort_block(0, t)
    for t in sides:
        send_block(0, t, 0)
    for t in near:
        sort_block(0, t)
    for t in far:
        sort_block(1, t)
    drain(plane_in, g_recv.at[0])
    drain(plane_in, g_send.at[0])
    mine = pl.ds(place * plane_rows, plane_rows)
    gbuf[:, mine] += plane_in[0] + plane_in[1] + plane_in[2]

    for t in sides[:1]:
        sort_block(1, t)
    for o in range(1, lines):
        theirs = pl.ds(place * plane_rows + ((line + o) % lines) * line_rows, line_rows)
        stage(1, gbuf.at[:, theirs], line_in.at[o - 1], line_peer(o))
    for t in sides:
        send_block(0, t, 1)
    for t in near:
        send_block(0, t)
    for t in sides[1:] + near:
        sort_block(1, t)
    drain(line_in, g_recv.at[1])
    drain(line_in, g_send.at[1])
    own = pl.ds(place * plane_rows + line * line_rows, line_rows)
    total = gbuf[:, own]
    for o in range(1, lines):
        total = total + line_in[o - 1]
    gall[:, own] = total
    lax.fori_loop(0, count // 256, build_pick, 0)

    for o in range(1, lines):
        stage(2, gall.at[:, own], gall.at[:, own], line_peer(o))
    for t in far:
        send_block(1, t)
    drain(line_in, g_recv.at[2])
    drain(line_in, g_send.at[2])
    for o in range(1, PLANE):
        stage(3, gall.at[:, mine], gall.at[:, mine], plane_peer(o))
    for t in sides + near:
        send_block(1, t)

    drain(rbuf.at[0], bulk_recv.at[0])
    attend_block(0, turns[0])
    for a, b in zip(turns[1:], turns[:-1]):
        attend_block(0, a)
        return_block(0, b)
    return_block(0, turns[-1])
    drain(plane_in, g_recv.at[3])
    drain(plane_in, g_send.at[3])

    u_buf[0] = renewed(w1_ref[...], gall[0])
    u_buf[1] = renewed(w3_ref[...], gall[1])
    u_buf[2] = renewed(w2_ref[...], jnp.transpose(gall[2]))

    def readout(i, c):
        step = 256
        here = pl.ds(pl.multiple_of(i * step, step), step)
        query = q_ref[here]
        q1, q3 = nt(query, u_buf[0]), nt(query, u_buf[1])
        act = (q1 * jax.nn.sigmoid(q1) * q3).astype(BF16)
        y = nt(act, u_buf[2])
        y_buf[here] = y
        half = y[:, :128] * y[:, :128] + y[:, 128:] * y[:, 128:]
        for b in range(step // 128):
            part = jnp.sum(jnp.transpose(half[b * 128 : (b + 1) * 128]), axis=0, keepdims=True)
            sq_own[pl.ds(i * (step // 128) + b, 1)] = part
        return c

    lax.fori_loop(0, count // 256, readout, 0)

    def send_sq(o, c):
        pltpu.make_async_remote_copy(
            src_ref=sq_own, dst_ref=sq_in.at[o - 1], send_sem=sq_send, recv_sem=sq_recv,
            device_id=(cam, (head + o) % heads), device_id_type=MESH,
        ).start()
        return c

    drain(rbuf.at[1], bulk_recv.at[1])
    attend_block(1, turns[0])
    lax.fori_loop(1, heads, send_sq, 0)
    for a, b in zip(turns[1:], turns[:-1]):
        attend_block(1, a)
        return_block(1, b)
    return_block(1, turns[-1])

    drain(ret.at[0], back_recv.at[0])

    def first_half(i, c):
        here = pl.ds(pl.multiple_of(i * 256, 256), 256)
        acc[here] = nn(pick_of(0, here, 256), ret[0].reshape(frame_rows, width))
        return c

    lax.fori_loop(0, count // 256, first_half, 0)

    drain(sq_in, sq_send)
    drain(sq_in, sq_recv)
    square = sq_own[...]
    for o in range(1, heads):
        square = square + sq_in[o - 1]
    sq_own[...] = 1.0 / jnp.sqrt(square / (width * heads) + EPSILON)

    def scaled(b, c):
        here = pl.ds(pl.multiple_of(b * 128, 128), 128)
        inv = column_of(sq_own[pl.ds(b, 1)])
        acc[here] += y_buf[here] * jnp.concatenate([inv, inv], axis=1) * gain_ref[...]
        return c

    lax.fori_loop(0, count // 128, scaled, 0)
    drain(ret.at[1], back_recv.at[1])

    def second_half(i, c):
        here = pl.ds(pl.multiple_of(i * 256, 256), 256)
        taken = nn(pick_b[here], ret[1].reshape(frame_rows, width))
        out_ref[here] = (acc[here] + taken).astype(BF16)
        pltpu.make_async_copy(out_ref.at[here], out_hbm.at[here], out_sem).start()
        return c

    lax.fori_loop(0, count // 256, second_half, 0)
    drain(out_ref, out_sem)
    for frame in range(2):
        drain(sbuf.at[frame, pl.ds(0, cams - 1)], bulk_send.at[frame])
        drain(obuf.at[frame, pl.ds(0, cams - 1)], back_send.at[frame])


def per_device(cams, heads, queries, keys, values, rates, w_one, w_three, w_two, gain, order):
    count, width = queries.shape
    hid = w_one.shape[1]
    plane_rows = hid // PLANE
    lines = cams // PLANE
    line_rows = plane_rows // lines
    dma = pltpu.SemaphoreType.DMA
    hbm = pl.BlockSpec(memory_space=pl.ANY)
    return pl.pallas_call(
        functools.partial(layer, cams, heads),
        out_shape=jax.ShapeDtypeStruct((count, width), BF16),
        in_specs=[hbm] * 9,
        out_specs=hbm,
        scratch_shapes=[
            pltpu.VMEM((count, width), BF16),
            pltpu.VMEM((count, width), BF16),
            pltpu.VMEM((count, width), BF16),
            pltpu.VMEM((1, count), F32),
            pltpu.VMEM((hid, width), BF16),
            pltpu.VMEM((hid, width), BF16),
            pltpu.VMEM((width, hid), BF16),
            pltpu.VMEM((1, width), F32),
            pltpu.VMEM((1, count), jnp.int32),
            pltpu.VMEM((count, width), BF16),
            pltpu.VMEM((count, width), F32),
            pltpu.VMEM((count, cams * PATCHES), BF16),
            pltpu.VMEM((2, cams, 3, PATCHES, width), BF16),
            pltpu.VMEM((2, cams, 3, PATCHES, width), BF16),
            pltpu.VMEM((2, cams, PATCHES, width), BF16),
            pltpu.VMEM((2, cams, PATCHES, width), BF16),
            pltpu.VMEM((3, hid, width), F32),
            pltpu.VMEM((3, hid, width), F32),
            pltpu.VMEM((PLANE - 1, 3, plane_rows, width), F32),
            pltpu.VMEM((lines - 1, 3, line_rows, width), F32),
            pltpu.VMEM((3, hid, width), BF16),
            pltpu.VMEM((count, width), F32),
            pltpu.VMEM((count, 128), F32),
            pltpu.VMEM((count, 128), F32),
            pltpu.VMEM((count // 128, 128), F32),
            pltpu.VMEM((heads - 1, count // 128, 128), F32),
            dma((2,)),
            dma((2,)),
            dma((2,)),
            dma((2,)),
            dma((4,)),
            dma((4,)),
            dma,
            dma,
            dma((9,)),
            dma,
        ],
        compiler_params=pltpu.CompilerParams(
            collective_id=0, has_side_effects=True, vmem_limit_bytes=60 * 1024 * 1024
        ),
        name="layer",
    )(
        queries, keys, values, rates.reshape(1, count),
        w_one[0], w_three[0], w_two[0], gain.reshape(1, width), order,
    )


def solution(mesh):
    in_specs = (
        P("cam", "head"),
        P("cam", "head"),
        P("cam", "head"),
        P("cam", "head"),
        P("head", None, None),
        P("head", None, None),
        P("head", None, None),
        P("head"),
        P("cam", None),
    )
    step = functools.partial(per_device, mesh.shape["cam"], mesh.shape["head"])
    return jax.shard_map(
        step, mesh=mesh, in_specs=in_specs, out_specs=P("cam", "head"), check_vma=False
    )
```

```python
import functools
import jax
import jax.numpy as jnp
from jax import lax
from jax.experimental import pallas as pl
from jax.experimental.pallas import tpu as pltpu
from jax.sharding import PartitionSpec as P

PATCHES = 32
EPSILON = 1e-06
GROUP = 8
PLANE = 4
MESH = pl.DeviceIdType.MESH
F32 = jnp.float32
BF16 = jnp.bfloat16


def nt(a, b):
    return lax.dot_general(a, b, (((1,), (1,)), ((), ())), preferred_element_type=F32)


def nn(a, b):
    return jnp.dot(a, b, preferred_element_type=F32)


def column_of(row):
    return jnp.transpose(jnp.broadcast_to(row, (128, 128)))


def drain(ref, sem):
    pltpu.make_async_copy(ref, ref, sem).wait()


def mean_square(weight):
    wf = weight.astype(F32)
    return jnp.mean(wf * wf)


def renewed(rows, grad, weight_square, grad_square):
    scale = jnp.sqrt(weight_square) / jnp.sqrt(grad_square + EPSILON)
    moved = rows - scale * grad
    ratio = jnp.sqrt(jnp.sum(rows * rows, axis=1, keepdims=True)) / jnp.sqrt(
        jnp.sum(moved * moved, axis=1, keepdims=True) + EPSILON
    )
    return moved * ratio


def layer(
    cams, heads,
    q_hbm, k_hbm, v_hbm, rates_hbm, w1_hbm, w3_hbm, w2_hbm, gain_hbm, order_hbm,
    out_ref,
    q_ref, k_ref, v_ref, rates_ref, w1_ref, w3_ref, w2_ref, gain_ref, order_ref,
    acc, pick_b, w32, line_own, sums_own, sums_in, sbuf, rbuf, obuf, ret, gbuf, gall, plane_in, line_in, u_buf, y_buf,
    rcol, ocol, sq_own, sq_in,
    bulk_send, bulk_recv, back_send, back_recv,
    g_send, g_recv, sq_send, sq_recv, in_sem, sums_send, sums_recv,
):
    count, width = q_ref.shape
    lines = cams // PLANE
    blocks = cams // GROUP
    rows = GROUP * PATCHES
    frame_rows = cams * PATCHES
    hid = w1_ref.shape[0]
    plane_rows = hid // PLANE
    line_rows = plane_rows // lines
    cam = lax.axis_index("cam")
    head = lax.axis_index("head")
    line, place = cam // PLANE, cam % PLANE

    def load(n, src, dst):
        copy = pltpu.make_async_copy(src, dst, in_sem.at[n])
        copy.start()
        return copy

    early = [
        load(n, src, dst)
        for n, (src, dst) in enumerate(
            ((order_hbm, order_ref), (q_hbm, q_ref), (k_hbm, k_ref), (v_hbm, v_ref))
        )
    ]
    barrier = pltpu.get_barrier_semaphore()

    def greet_cam(o, c):
        pl.semaphore_signal(
            barrier, inc=1, device_id=((cam + o) % cams, head), device_id_type=MESH
        )
        return c

    def greet_head(o, c):
        pl.semaphore_signal(
            barrier, inc=1, device_id=(cam, (head + o) % heads), device_id_type=MESH
        )
        return c

    lax.fori_loop(1, cams, greet_cam, 0)
    lax.fori_loop(1, heads, greet_head, 0)

    later = [
        load(n + 4, src, dst)
        for n, (src, dst) in enumerate(
            (
                (rates_hbm, rates_ref), (w1_hbm, w1_ref), (w3_hbm, w3_ref),
                (w2_hbm, w2_ref), (gain_hbm, gain_ref),
            )
        )
    ]

    def block_at(turn):
        return (cam // GROUP + turn) % blocks

    def sort_block(frame, turn):
        blk = block_at(turn)
        first = frame * frame_rows + blk * rows
        slot = lax.broadcasted_iota(jnp.int32, (rows, count), 0) + first
        pick = jnp.where(slot == order_ref[...], 1.0, 0.0).astype(BF16)
        for a, ref in enumerate((q_ref, k_ref, v_ref)):
            got = nn(pick, ref[...]).astype(BF16).reshape(GROUP, PATCHES, width)
            sbuf[frame, pl.ds(blk * GROUP, GROUP), a] = got

    def send_block(frame, turn, half=None):
        blk = block_at(turn)
        low = 1 if turn == 0 else 0
        low, high = {None: (low, GROUP), 0: (low, GROUP // 2), 1: (GROUP // 2, GROUP)}[half]

        def one(j, c):
            dest = blk * GROUP + (cam + j) % GROUP
            pltpu.make_async_remote_copy(
                src_ref=sbuf.at[frame, dest],
                dst_ref=rbuf.at[frame, cam],
                send_sem=bulk_send.at[frame],
                recv_sem=bulk_recv.at[frame],
                device_id=(dest, head),
                device_id_type=MESH,
            ).start()
            return c

        if turn == 0 and half != 1:
            pltpu.make_async_copy(
                sbuf.at[frame, cam], rbuf.at[frame, cam], bulk_recv.at[frame]
            ).start()
        lax.fori_loop(low, high, one, 0)

    def attend_block(frame, turn):
        blk = block_at(turn)
        query = rbuf[frame, pl.ds(blk * GROUP, GROUP), 0].reshape(rows, width)
        key = rbuf[frame, :, 1].reshape(frame_rows, width)
        value = rbuf[frame, :, 2].reshape(frame_rows, width)
        scores = nt(query, key) * (width ** (-0.5))
        expo = jnp.exp(scores - jnp.max(scores, axis=1, keepdims=True))
        probs = (expo * (1.0 / jnp.sum(expo, axis=1, keepdims=True))).astype(BF16)
        got = nn(probs, value).astype(BF16).reshape(GROUP, PATCHES, width)
        obuf[frame, pl.ds(blk * GROUP, GROUP)] = got

    def return_block(frame, turn):
        blk = block_at(turn)

        def one(j, c):
            dest = blk * GROUP + (cam + j) % GROUP
            pltpu.make_async_remote_copy(
                src_ref=obuf.at[frame, dest],
                dst_ref=ret.at[frame, cam],
                send_sem=back_send.at[frame],
                recv_sem=back_recv.at[frame, turn],
                device_id=(dest, head),
                device_id_type=MESH,
            ).start()
            return c

        if turn == 0:
            pltpu.make_async_copy(
                obuf.at[frame, cam], ret.at[frame, cam], back_recv.at[frame, turn]
            ).start()
        lax.fori_loop(1 if turn == 0 else 0, GROUP, one, 0)

    turns = [t for t in (2, 1, 3, 0) if t < blocks]

    def columns(b, c):
        lanes = pl.ds(pl.multiple_of(b * 128, 128), 128)
        here = pl.ds(pl.multiple_of(b * 128, 128), 128)
        rcol[here] = column_of(rates_ref[:, lanes])
        ocol[here] = column_of(order_ref[:, lanes].astype(F32))
        return c

    def grad_step(i, c):
        step = 512
        here = pl.ds(pl.multiple_of(i * step, step), step)
        key, val = k_ref[here], v_ref[here].astype(F32)
        rate = rcol[here]
        err = (-jnp.concatenate([rate, rate], axis=1) * val).astype(BF16)
        a1, a3 = nt(w1_ref[...], key), nt(w3_ref[...], key)
        s = jax.nn.sigmoid(a1)
        act = (a1 * s * a3).astype(BF16)
        back = nt(u_buf[0], err)
        b1 = (back * a3 * s * (1.0 + a1 * (1.0 - s))).astype(BF16)
        b3 = (back * a1 * s).astype(BF16)
        gbuf[0] += nn(b1, key)
        gbuf[1] += nn(b3, key)
        gbuf[2] += nn(act, err)
        return c

    def pick_of(frame, here, step):
        at = ocol[here]
        lane = lax.broadcasted_iota(jnp.int32, (step, 128), 1).astype(F32)
        return jnp.concatenate(
            [
                jnp.where(at == lane + float(frame * frame_rows + b), 1.0, 0.0).astype(BF16)
                for b in range(0, frame_rows, 128)
            ],
            axis=1,
        )

    def build_pick(i, c):
        here = pl.ds(pl.multiple_of(i * 256, 256), 256)
        pick = pick_of(1, here, 256)
        for b in range(blocks):
            pick_b[b, here] = pick[:, b * rows : (b + 1) * rows]
        return c

    def plane_peer(o):
        return (line * PLANE + (place + o) % PLANE, head)

    def line_peer(o):
        return (((line + o) % lines) * PLANE + place, head)

    def stage(n, src, dst, peer):
        pltpu.make_async_remote_copy(
            src_ref=src, dst_ref=dst, send_sem=g_send.at[n], recv_sem=g_recv.at[n],
            device_id=peer, device_id_type=MESH,
        ).start()

    far, sides, near = turns[:1], turns[1:-1], turns[-1:]
    if len(turns) == 1:
        far, near = turns, []

    for copy in early:
        copy.wait()
    for t in far:
        sort_block(0, t)
    pl.semaphore_wait(barrier, cams - 1 + heads - 1)
    for t in far:
        send_block(0, t)

    for copy in later:
        copy.wait()
    lax.fori_loop(0, count // 128, columns, 0)
    for m, w in enumerate((w1_ref, w3_ref, w2_ref)):
        w32[m] = w[...].astype(F32)
    u_buf[0] = jnp.transpose(w32[2]).astype(BF16)
    gbuf[...] = jnp.zeros_like(gbuf)
    lax.fori_loop(0, count // 512, grad_step, 0)
    gbuf[2] = jnp.transpose(gbuf[2])
    for t in sides[:1]:
        sort_block(0, t)
    for o in range(1, PLANE):
        theirs = pl.ds(((place + o) % PLANE) * plane_rows, plane_rows)
        stage(0, gbuf.at[:, theirs], plane_in.at[o - 1], plane_peer(o))
    for t in sides[1:]:
        sort_block(0, t)
    for t in sides:
        send_block(0, t, 0)
    for t in near:
        sort_block(0, t)
    for t in far:
        sort_block(1, t)
    drain(plane_in, g_recv.at[0])
    drain(plane_in, g_send.at[0])
    mine = pl.ds(place * plane_rows, plane_rows)
    gbuf[:, mine] += plane_in[0] + plane_in[1] + plane_in[2]

    for t in sides[:1]:
        sort_block(1, t)
    for o in range(1, lines):
        theirs = pl.ds(place * plane_rows + ((line + o) % lines) * line_rows, line_rows)
        stage(1, gbuf.at[:, theirs], line_in.at[o - 1], line_peer(o))
    for t in sides:
        send_block(0, t, 1)
    for t in near:
        send_block(0, t)
    for t in far:
        send_block(1, t, 0)
    for t in sides[1:] + near:
        sort_block(1, t)
    drain(line_in, g_recv.at[1])
    drain(line_in, g_send.at[1])
    own = pl.ds(place * plane_rows + line * line_rows, line_rows)
    total = gbuf[:, own]
    for o in range(1, lines):
        total = total + line_in[o - 1]
    lane = lax.broadcasted_iota(jnp.int32, (1, 128), 1)
    squares = jnp.zeros((1, 128), F32)
    for m in range(3):
        squares = jnp.where(lane == m, jnp.sum(total[m] * total[m]), squares)
    sums_own[...] = squares
    line_own[...] = total

    def send_sums(o, c):
        pltpu.make_async_remote_copy(
            src_ref=sums_own, dst_ref=sums_in.at[o - 1],
            send_sem=sums_send, recv_sem=sums_recv,
            device_id=((cam + o) % cams, head), device_id_type=MESH,
        ).start()
        return c

    lax.fori_loop(0, count // 256, build_pick, 0)
    lax.fori_loop(1, cams, send_sums, 0)
    for t in far:
        send_block(1, t, 1)
    for t in sides:
        send_block(1, t, 0)
    weight_squares = [mean_square(w[...]) for w in (w1_ref, w3_ref, w2_ref)]
    drain(sums_in, sums_recv)
    drain(sums_in, sums_send)
    squares = sums_own[...] + jnp.sum(sums_in[...], axis=0)
    for m, w in enumerate((w1_ref, w3_ref, w2_ref)):
        square = jnp.sum(jnp.where(lane == m, squares, 0.0)) / (hid * width)
        piece = renewed(w32[m, own], line_own[m], weight_squares[m], square)
        gall[place, line, m] = jnp.concatenate(
            [piece[:, :128], piece[:, 128:]], axis=0
        ).astype(BF16)

    for o in range(1, lines):
        stage(2, gall.at[place, line], gall.at[place, line], line_peer(o))
    for t in sides:
        send_block(1, t, 1)
    drain(gall.at[0, pl.ds(0, lines - 1)], g_recv.at[2])
    drain(gall.at[0, pl.ds(0, lines - 1)], g_send.at[2])
    for o in range(1, PLANE):
        stage(3, gall.at[place], gall.at[place], plane_peer(o))
    for t in near:
        send_block(1, t)

    drain(rbuf.at[0], bulk_recv.at[0])
    attend_block(0, turns[0])
    for a, b in zip(turns[1:], turns[:-1]):
        attend_block(0, a)
        return_block(0, b)
    return_block(0, turns[-1])

    drain(rbuf.at[1], bulk_recv.at[1])
    attend_block(1, turns[0])
    for a, b in zip(turns[1:], turns[:-1]):
        attend_block(1, a)
        return_block(1, b)
    return_block(1, turns[-1])

    drain(gall.at[pl.ds(0, PLANE - 1)], g_recv.at[3])
    drain(gall.at[pl.ds(0, PLANE - 1)], g_send.at[3])
    for m in range(3):
        for p in range(PLANE):
            for n in range(lines):
                at = pl.ds(p * plane_rows + n * line_rows, line_rows)
                piece = gall[p, n, m].astype(F32)
                gbuf[m, at] = jnp.concatenate([piece[:line_rows], piece[line_rows:]], axis=1)
    u_buf[...] = gbuf[...].astype(BF16)

    def readout(i, c):
        step = 256
        here = pl.ds(pl.multiple_of(i * step, step), step)
        query = q_ref[here]
        q1, q3 = nt(query, u_buf[0]), nt(query, u_buf[1])
        act = (q1 * jax.nn.sigmoid(q1) * q3).astype(BF16)
        y = nt(act, u_buf[2])
        y_buf[here] = y * gain_ref[...]
        half = y[:, :128] * y[:, :128] + y[:, 128:] * y[:, 128:]
        for b in range(step // 128):
            part = jnp.sum(jnp.transpose(half[b * 128 : (b + 1) * 128]), axis=0, keepdims=True)
            sq_own[pl.ds(i * (step // 128) + b, 1)] = part
        return c

    lax.fori_loop(0, count // 256, readout, 0)

    def send_sq(o, c):
        pltpu.make_async_remote_copy(
            src_ref=sq_own, dst_ref=sq_in.at[o - 1], send_sem=sq_send, recv_sem=sq_recv,
            device_id=(cam, (head + o) % heads), device_id_type=MESH,
        ).start()
        return c

    lax.fori_loop(1, heads, send_sq, 0)

    def owners_at(turn):
        return (cam // GROUP - turn) % blocks

    def await_return(frame, turn):
        drain(ret.at[frame, pl.ds(owners_at(turn) * GROUP, GROUP)], back_recv.at[frame, turn])

    for t in turns:
        await_return(0, t)

    def first_half(i, c):
        here = pl.ds(pl.multiple_of(i * 256, 256), 256)
        acc[here] = nn(pick_of(0, here, 256), ret[0].reshape(frame_rows, width))
        return c

    lax.fori_loop(0, count // 256, first_half, 0)

    drain(sq_in, sq_send)
    drain(sq_in, sq_recv)
    square = sq_own[...]
    for o in range(1, heads):
        square = square + sq_in[o - 1]
    sq_own[...] = 1.0 / jnp.sqrt(square / (width * heads) + EPSILON)

    def scaled(b, c):
        here = pl.ds(pl.multiple_of(b * 128, 128), 128)
        rcol[here] = column_of(sq_own[pl.ds(b, 1)])
        return c

    lax.fori_loop(0, count // 128, scaled, 0)

    for t in turns:
        await_return(1, t)

    def second_half(i, c):
        here = pl.ds(pl.multiple_of(i * 512, 512), 512)
        inv = rcol[here]
        got = acc[here] + y_buf[here] * jnp.concatenate([inv, inv], axis=1)
        for b in range(blocks):
            got += nn(pick_b[b, here], ret[1, b * GROUP : (b + 1) * GROUP].reshape(rows, width))
        out_ref[here] = got.astype(BF16)
        return c

    lax.fori_loop(0, count // 512, second_half, 0)
    for frame in range(2):
        drain(sbuf.at[frame, pl.ds(0, cams - 1)], bulk_send.at[frame])
        drain(obuf.at[frame, pl.ds(0, cams - 1)], back_send.at[frame])


def per_device(cams, heads, queries, keys, values, rates, w_one, w_three, w_two, gain, order):
    count, width = queries.shape
    hid = w_one.shape[1]
    plane_rows = hid // PLANE
    lines = cams // PLANE
    line_rows = plane_rows // lines
    dma = pltpu.SemaphoreType.DMA
    hbm = pl.BlockSpec(memory_space=pl.ANY)
    return pl.pallas_call(
        functools.partial(layer, cams, heads),
        out_shape=pltpu.VMEM((count, width), BF16),
        in_specs=[hbm] * 9,
        out_specs=pl.BlockSpec(memory_space=pltpu.VMEM),
        scratch_shapes=[
            pltpu.VMEM((count, width), BF16),
            pltpu.VMEM((count, width), BF16),
            pltpu.VMEM((count, width), BF16),
            pltpu.VMEM((1, count), F32),
            pltpu.VMEM((hid, width), BF16),
            pltpu.VMEM((hid, width), BF16),
            pltpu.VMEM((width, hid), BF16),
            pltpu.VMEM((1, width), F32),
            pltpu.VMEM((1, count), jnp.int32),
            pltpu.VMEM((count, width), F32),
            pltpu.VMEM((cams // GROUP, count, GROUP * PATCHES), BF16),
            pltpu.VMEM((3, hid, width), F32),
            pltpu.VMEM((3, line_rows, width), F32),
            pltpu.VMEM((1, 128), F32),
            pltpu.VMEM((cams - 1, 1, 128), F32),
            pltpu.VMEM((2, cams, 3, PATCHES, width), BF16),
            pltpu.VMEM((2, cams, 3, PATCHES, width), BF16),
            pltpu.VMEM((2, cams, PATCHES, width), BF16),
            pltpu.VMEM((2, cams, PATCHES, width), BF16),
            pltpu.VMEM((3, hid, width), F32),
            pltpu.VMEM((PLANE, lines, 3, 2 * line_rows, width // 2), BF16),
            pltpu.VMEM((PLANE - 1, 3, plane_rows, width), F32),
            pltpu.VMEM((lines - 1, 3, line_rows, width), F32),
            pltpu.VMEM((3, hid, width), BF16),
            pltpu.VMEM((count, width), F32),
            pltpu.VMEM((count, 128), F32),
            pltpu.VMEM((count, 128), F32),
            pltpu.VMEM((count // 128, 128), F32),
            pltpu.VMEM((heads - 1, count // 128, 128), F32),
            dma((2,)),
            dma((2,)),
            dma((2,)),
            dma((2, cams // GROUP)),
            dma((4,)),
            dma((4,)),
            dma,
            dma,
            dma((9,)),
            dma,
            dma,
        ],
        compiler_params=pltpu.CompilerParams(
            collective_id=0, has_side_effects=True, vmem_limit_bytes=60 * 1024 * 1024
        ),
        name="layer",
    )(
        queries, keys, values, rates.reshape(1, count),
        w_one[0], w_three[0], w_two[0], gain.reshape(1, width), order,
    )


def solution(mesh):
    in_specs = (
        P("cam", "head"),
        P("cam", "head"),
        P("cam", "head"),
        P("cam", "head"),
        P("head", None, None),
        P("head", None, None),
        P("head", None, None),
        P("head"),
        P("cam", None),
    )
    step = functools.partial(per_device, mesh.shape["cam"], mesh.shape["head"])
    return jax.shard_map(
        step, mesh=mesh, in_specs=in_specs, out_specs=P("cam", "head"), check_vma=False
    )
```

```python
import functools
import jax
import jax.numpy as jnp
from jax import lax
from jax.experimental import pallas as pl
from jax.experimental.pallas import tpu as pltpu
from jax.sharding import PartitionSpec as P

PATCHES = 32
EPSILON = 1e-06
GROUP = 8
PLANE = 4
MESH = pl.DeviceIdType.MESH
F32 = jnp.float32
BF16 = jnp.bfloat16


def nt(a, b):
    return lax.dot_general(a, b, (((1,), (1,)), ((), ())), preferred_element_type=F32)


def nn(a, b):
    return jnp.dot(a, b, preferred_element_type=F32)


def column_of(row):
    return jnp.transpose(jnp.broadcast_to(row, (128, 128)))


def drain(ref, sem):
    pltpu.make_async_copy(ref, ref, sem).wait()


def mean_square(weight):
    wf = weight.astype(F32)
    return jnp.mean(wf * wf)


def renewed(rows, grad, weight_square, grad_square):
    scale = jnp.sqrt(weight_square) / jnp.sqrt(grad_square + EPSILON)
    moved = rows - scale * grad
    ratio = jnp.sqrt(jnp.sum(rows * rows, axis=1, keepdims=True)) / jnp.sqrt(
        jnp.sum(moved * moved, axis=1, keepdims=True) + EPSILON
    )
    return moved * ratio


def layer(
    cams, heads,
    q_hbm, k_hbm, v_hbm, rates_hbm, w1_hbm, w3_hbm, w2_hbm, gain_hbm, order_hbm,
    out_ref,
    q_ref, k_ref, v_ref, rates_ref, w1_ref, w3_ref, w2_ref, gain_ref, order_ref,
    acc, pick_b, w32, line_own, sums_own, sums_in, sbuf, rbuf, obuf, ret, gbuf, gall, plane_in, line_in, u_buf, y_buf,
    rcol, ocol, sq_own, sq_in,
    bulk_send, bulk_recv, back_send, back_recv,
    g_send, g_recv, sq_send, sq_recv, in_sem, sums_send, sums_recv,
):
    count, width = q_ref.shape
    lines = cams // PLANE
    blocks = cams // GROUP
    rows = GROUP * PATCHES
    frame_rows = cams * PATCHES
    hid = w1_ref.shape[0]
    plane_rows = hid // PLANE
    line_rows = plane_rows // lines
    cam = lax.axis_index("cam")
    head = lax.axis_index("head")
    line, place = cam // PLANE, cam % PLANE

    def load(n, src, dst):
        copy = pltpu.make_async_copy(src, dst, in_sem.at[n])
        copy.start()
        return copy

    early = [
        load(n, src, dst)
        for n, (src, dst) in enumerate(
            ((order_hbm, order_ref), (q_hbm, q_ref), (k_hbm, k_ref), (v_hbm, v_ref))
        )
    ]
    barrier = pltpu.get_barrier_semaphore()

    def greet_cam(o, c):
        peer = (cam + cams // 2 + o) % cams
        pl.semaphore_signal(barrier, inc=1, device_id=(peer, head), device_id_type=MESH)
        return c

    def greet_head(o, c):
        pl.semaphore_signal(
            barrier, inc=1, device_id=(cam, (head + o) % heads), device_id_type=MESH
        )
        return c

    lax.fori_loop(0, cams // 2, greet_cam, 0)
    lax.fori_loop(cams // 2 + 1, cams, greet_cam, 0)
    lax.fori_loop(1, heads, greet_head, 0)

    later = [
        load(n + 4, src, dst)
        for n, (src, dst) in enumerate(
            (
                (rates_hbm, rates_ref), (w1_hbm, w1_ref), (w3_hbm, w3_ref),
                (w2_hbm, w2_ref), (gain_hbm, gain_ref),
            )
        )
    ]

    def block_at(turn):
        return (cam // GROUP + turn) % blocks

    def sort_block(frame, turn, arriving=(None, None, None)):
        blk = block_at(turn)
        first = frame * frame_rows + blk * rows
        slot = lax.broadcasted_iota(jnp.int32, (rows, count), 0) + first
        pick = jnp.where(slot == order_ref[...], 1.0, 0.0).astype(BF16)
        for a, ref in enumerate((q_ref, k_ref, v_ref)):
            if arriving[a] is not None:
                arriving[a].wait()
            got = nn(pick, ref[...]).astype(BF16).reshape(GROUP, PATCHES, width)
            sbuf[frame, pl.ds(blk * GROUP, GROUP), a] = got

    def send_block(frame, turn, half=None):
        blk = block_at(turn)
        low = 1 if turn == 0 else 0
        low, high = {None: (low, GROUP), 0: (low, GROUP // 2), 1: (GROUP // 2, GROUP)}[half]

        def one(j, c):
            dest = blk * GROUP + (cam + j) % GROUP
            pltpu.make_async_remote_copy(
                src_ref=sbuf.at[frame, dest],
                dst_ref=rbuf.at[frame, cam],
                send_sem=bulk_send.at[frame],
                recv_sem=bulk_recv.at[frame],
                device_id=(dest, head),
                device_id_type=MESH,
            ).start()
            return c

        if turn == 0 and half != 1:
            pltpu.make_async_copy(
                sbuf.at[frame, cam], rbuf.at[frame, cam], bulk_recv.at[frame]
            ).start()
        lax.fori_loop(low, high, one, 0)

    def attend_block(frame, turn):
        blk = block_at(turn)
        query = rbuf[frame, pl.ds(blk * GROUP, GROUP), 0].reshape(rows, width)
        key = rbuf[frame, :, 1].reshape(frame_rows, width)
        value = rbuf[frame, :, 2].reshape(frame_rows, width)
        scores = nt(query, key) * (width ** (-0.5))
        expo = jnp.exp(scores - jnp.max(scores, axis=1, keepdims=True))
        probs = (expo * (1.0 / jnp.sum(expo, axis=1, keepdims=True))).astype(BF16)
        got = nn(probs, value).astype(BF16).reshape(GROUP, PATCHES, width)
        obuf[frame, pl.ds(blk * GROUP, GROUP)] = got

    def return_block(frame, turn):
        blk = block_at(turn)

        def one(j, c):
            dest = blk * GROUP + (cam + j) % GROUP
            pltpu.make_async_remote_copy(
                src_ref=obuf.at[frame, dest],
                dst_ref=ret.at[frame, cam],
                send_sem=back_send.at[frame],
                recv_sem=back_recv.at[frame, turn],
                device_id=(dest, head),
                device_id_type=MESH,
            ).start()
            return c

        if turn == 0:
            pltpu.make_async_copy(
                obuf.at[frame, cam], ret.at[frame, cam], back_recv.at[frame, turn]
            ).start()
        lax.fori_loop(1 if turn == 0 else 0, GROUP, one, 0)

    turns = [t for t in (2, 1, 3, 0) if t < blocks]

    def columns(b, c):
        lanes = pl.ds(pl.multiple_of(b * 128, 128), 128)
        here = pl.ds(pl.multiple_of(b * 128, 128), 128)
        rcol[here] = column_of(rates_ref[:, lanes])
        ocol[here] = column_of(order_ref[:, lanes].astype(F32))
        return c

    def grad_step(i, c):
        step = 512
        here = pl.ds(pl.multiple_of(i * step, step), step)
        key, val = k_ref[here], v_ref[here].astype(F32)
        rate = rcol[here]
        err = (-jnp.concatenate([rate, rate], axis=1) * val).astype(BF16)
        a1, a3 = nt(w1_ref[...], key), nt(w3_ref[...], key)
        s = jax.nn.sigmoid(a1)
        act = (a1 * s * a3).astype(BF16)
        back = nt(u_buf[0], err)
        b1 = (back * a3 * s * (1.0 + a1 * (1.0 - s))).astype(BF16)
        b3 = (back * a1 * s).astype(BF16)
        gbuf[0] += nn(b1, key)
        gbuf[1] += nn(b3, key)
        gbuf[2] += nn(act, err)
        return c

    def pick_of(frame, here, step):
        at = ocol[here]
        lane = lax.broadcasted_iota(jnp.int32, (step, 128), 1).astype(F32)
        return jnp.concatenate(
            [
                jnp.where(at == lane + float(frame * frame_rows + b), 1.0, 0.0).astype(BF16)
                for b in range(0, frame_rows, 128)
            ],
            axis=1,
        )

    def build_pick(i, c):
        here = pl.ds(pl.multiple_of(i * 256, 256), 256)
        pick = pick_of(1, here, 256)
        for b in range(blocks):
            pick_b[b, here] = pick[:, b * rows : (b + 1) * rows]
        return c

    def plane_peer(o):
        return (line * PLANE + (place + o) % PLANE, head)

    def line_peer(o):
        return (((line + o) % lines) * PLANE + place, head)

    def stage(n, src, dst, peer):
        pltpu.make_async_remote_copy(
            src_ref=src, dst_ref=dst, send_sem=g_send.at[n], recv_sem=g_recv.at[n],
            device_id=peer, device_id_type=MESH,
        ).start()

    far, sides, near = turns[:1], turns[1:-1], turns[-1:]
    if len(turns) == 1:
        far, near = turns, []

    early[0].wait()
    for t in far:
        sort_block(0, t, early[1:])
    pl.semaphore_wait(barrier, cams - 1 + heads - 1)
    for t in far:
        send_block(0, t)

    for copy in later:
        copy.wait()
    lax.fori_loop(0, count // 128, columns, 0)
    for m, w in enumerate((w1_ref, w3_ref, w2_ref)):
        w32[m] = w[...].astype(F32)
    u_buf[0] = jnp.transpose(w32[2]).astype(BF16)
    gbuf[...] = jnp.zeros_like(gbuf)
    lax.fori_loop(0, count // 512, grad_step, 0)
    gbuf[2] = jnp.transpose(gbuf[2])
    for t in sides[:1]:
        sort_block(0, t)
    for o in range(1, PLANE):
        theirs = pl.ds(((place + o) % PLANE) * plane_rows, plane_rows)
        stage(0, gbuf.at[:, theirs], plane_in.at[o - 1], plane_peer(o))
    for t in sides[1:]:
        sort_block(0, t)
    for t in sides:
        send_block(0, t, 0)
    for t in near:
        sort_block(0, t)
    for t in far:
        sort_block(1, t)
    drain(plane_in, g_recv.at[0])
    drain(plane_in, g_send.at[0])
    mine = pl.ds(place * plane_rows, plane_rows)
    gbuf[:, mine] += plane_in[0] + plane_in[1] + plane_in[2]

    for t in sides[:1]:
        sort_block(1, t)
    for o in range(1, lines):
        theirs = pl.ds(place * plane_rows + ((line + o) % lines) * line_rows, line_rows)
        stage(1, gbuf.at[:, theirs], line_in.at[o - 1], line_peer(o))
    for t in sides:
        send_block(0, t, 1)
    for t in near:
        send_block(0, t)
    for t in far:
        send_block(1, t, 0)
    for t in sides[1:] + near:
        sort_block(1, t)
    drain(line_in, g_recv.at[1])
    drain(line_in, g_send.at[1])
    own = pl.ds(place * plane_rows + line * line_rows, line_rows)
    total = gbuf[:, own]
    for o in range(1, lines):
        total = total + line_in[o - 1]
    lane = lax.broadcasted_iota(jnp.int32, (1, 128), 1)
    squares = jnp.zeros((1, 128), F32)
    for m in range(3):
        squares = jnp.where(lane == m, jnp.sum(total[m] * total[m]), squares)
    sums_own[...] = squares
    line_own[...] = total

    def send_sums(o, c):
        pltpu.make_async_remote_copy(
            src_ref=sums_own, dst_ref=sums_in.at[o - 1],
            send_sem=sums_send, recv_sem=sums_recv,
            device_id=((cam + o) % cams, head), device_id_type=MESH,
        ).start()
        return c

    lax.fori_loop(1, cams, send_sums, 0)
    for t in far:
        send_block(1, t, 1)
    for t in sides:
        send_block(1, t, 0)
    drain(rbuf.at[0], bulk_recv.at[0])
    for t in turns:
        attend_block(0, t)
    weight_squares = [mean_square(w[...]) for w in (w1_ref, w3_ref, w2_ref)]
    drain(sums_in, sums_recv)
    drain(sums_in, sums_send)
    squares = sums_own[...] + jnp.sum(sums_in[...], axis=0)
    for m, w in enumerate((w1_ref, w3_ref, w2_ref)):
        square = jnp.sum(jnp.where(lane == m, squares, 0.0)) / (hid * width)
        piece = renewed(w32[m, own], line_own[m], weight_squares[m], square)
        gall[place, line, m] = jnp.concatenate(
            [piece[:, :128], piece[:, 128:]], axis=0
        ).astype(BF16)

    for o in range(1, lines):
        stage(2, gall.at[place, line], gall.at[place, line], line_peer(o))
    for t in sides:
        send_block(1, t, 1)
    for t in near:
        send_block(1, t)
    for t in turns:
        return_block(0, t)
    drain(gall.at[0, pl.ds(0, lines - 1)], g_recv.at[2])
    drain(gall.at[0, pl.ds(0, lines - 1)], g_send.at[2])
    for o in range(1, PLANE):
        stage(3, gall.at[place], gall.at[place], plane_peer(o))
    lax.fori_loop(0, count // 256, build_pick, 0)

    drain(rbuf.at[1], bulk_recv.at[1])
    attend_block(1, turns[0])
    for a, b in zip(turns[1:], turns[:-1]):
        attend_block(1, a)
        return_block(1, b)
    return_block(1, turns[-1])

    drain(gall.at[pl.ds(0, PLANE - 1)], g_recv.at[3])
    drain(gall.at[pl.ds(0, PLANE - 1)], g_send.at[3])
    for m in range(3):
        for p in range(PLANE):
            for n in range(lines):
                at = pl.ds(p * plane_rows + n * line_rows, line_rows)
                piece = gall[p, n, m].astype(F32)
                gbuf[m, at] = jnp.concatenate([piece[:line_rows], piece[line_rows:]], axis=1)
    u_buf[...] = gbuf[...].astype(BF16)

    def readout(i, c):
        step = 256
        here = pl.ds(pl.multiple_of(i * step, step), step)
        query = q_ref[here]
        q1, q3 = nt(query, u_buf[0]), nt(query, u_buf[1])
        act = (q1 * jax.nn.sigmoid(q1) * q3).astype(BF16)
        y = nt(act, u_buf[2])
        y_buf[here] = y * gain_ref[...]
        half = y[:, :128] * y[:, :128] + y[:, 128:] * y[:, 128:]
        for b in range(step // 128):
            part = jnp.sum(jnp.transpose(half[b * 128 : (b + 1) * 128]), axis=0, keepdims=True)
            sq_own[pl.ds(i * (step // 128) + b, 1)] = part
        return c

    lax.fori_loop(0, count // 256, readout, 0)

    def send_sq(o, c):
        pltpu.make_async_remote_copy(
            src_ref=sq_own, dst_ref=sq_in.at[o - 1], send_sem=sq_send, recv_sem=sq_recv,
            device_id=(cam, (head + o) % heads), device_id_type=MESH,
        ).start()
        return c

    lax.fori_loop(1, heads, send_sq, 0)

    def owners_at(turn):
        return (cam // GROUP - turn) % blocks

    def await_return(frame, turn):
        drain(ret.at[frame, pl.ds(owners_at(turn) * GROUP, GROUP)], back_recv.at[frame, turn])

    for t in turns:
        await_return(0, t)

    def first_half(i, c):
        here = pl.ds(pl.multiple_of(i * 256, 256), 256)
        acc[here] = nn(pick_of(0, here, 256), ret[0].reshape(frame_rows, width))
        return c

    lax.fori_loop(0, count // 256, first_half, 0)

    drain(sq_in, sq_send)
    drain(sq_in, sq_recv)
    square = sq_own[...]
    for o in range(1, heads):
        square = square + sq_in[o - 1]
    sq_own[...] = 1.0 / jnp.sqrt(square / (width * heads) + EPSILON)

    def scaled(b, c):
        here = pl.ds(pl.multiple_of(b * 128, 128), 128)
        rcol[here] = column_of(sq_own[pl.ds(b, 1)])
        return c

    lax.fori_loop(0, count // 128, scaled, 0)

    for t in turns:
        await_return(1, t)

    def second_half(i, c):
        here = pl.ds(pl.multiple_of(i * 512, 512), 512)
        inv = rcol[here]
        got = acc[here] + y_buf[here] * jnp.concatenate([inv, inv], axis=1)
        for b in range(blocks):
            got += nn(pick_b[b, here], ret[1, b * GROUP : (b + 1) * GROUP].reshape(rows, width))
        out_ref[here] = got.astype(BF16)
        return c

    lax.fori_loop(0, count // 512, second_half, 0)
    for frame in range(2):
        drain(sbuf.at[frame, pl.ds(0, cams - 1)], bulk_send.at[frame])
        drain(obuf.at[frame, pl.ds(0, cams - 1)], back_send.at[frame])


def per_device(cams, heads, queries, keys, values, rates, w_one, w_three, w_two, gain, order):
    count, width = queries.shape
    hid = w_one.shape[1]
    plane_rows = hid // PLANE
    lines = cams // PLANE
    line_rows = plane_rows // lines
    dma = pltpu.SemaphoreType.DMA
    hbm = pl.BlockSpec(memory_space=pl.ANY)
    return pl.pallas_call(
        functools.partial(layer, cams, heads),
        out_shape=pltpu.VMEM((count, width), BF16),
        in_specs=[hbm] * 9,
        out_specs=pl.BlockSpec(memory_space=pltpu.VMEM),
        scratch_shapes=[
            pltpu.VMEM((count, width), BF16),
            pltpu.VMEM((count, width), BF16),
            pltpu.VMEM((count, width), BF16),
            pltpu.VMEM((1, count), F32),
            pltpu.VMEM((hid, width), BF16),
            pltpu.VMEM((hid, width), BF16),
            pltpu.VMEM((width, hid), BF16),
            pltpu.VMEM((1, width), F32),
            pltpu.VMEM((1, count), jnp.int32),
            pltpu.VMEM((count, width), F32),
            pltpu.VMEM((cams // GROUP, count, GROUP * PATCHES), BF16),
            pltpu.VMEM((3, hid, width), F32),
            pltpu.VMEM((3, line_rows, width), F32),
            pltpu.VMEM((1, 128), F32),
            pltpu.VMEM((cams - 1, 1, 128), F32),
            pltpu.VMEM((2, cams, 3, PATCHES, width), BF16),
            pltpu.VMEM((2, cams, 3, PATCHES, width), BF16),
            pltpu.VMEM((2, cams, PATCHES, width), BF16),
            pltpu.VMEM((2, cams, PATCHES, width), BF16),
            pltpu.VMEM((3, hid, width), F32),
            pltpu.VMEM((PLANE, lines, 3, 2 * line_rows, width // 2), BF16),
            pltpu.VMEM((PLANE - 1, 3, plane_rows, width), F32),
            pltpu.VMEM((lines - 1, 3, line_rows, width), F32),
            pltpu.VMEM((3, hid, width), BF16),
            pltpu.VMEM((count, width), F32),
            pltpu.VMEM((count, 128), F32),
            pltpu.VMEM((count, 128), F32),
            pltpu.VMEM((count // 128, 128), F32),
            pltpu.VMEM((heads - 1, count // 128, 128), F32),
            dma((2,)),
            dma((2,)),
            dma((2,)),
            dma((2, cams // GROUP)),
            dma((4,)),
            dma((4,)),
            dma,
            dma,
            dma((9,)),
            dma,
            dma,
        ],
        compiler_params=pltpu.CompilerParams(
            collective_id=0, has_side_effects=True, vmem_limit_bytes=60 * 1024 * 1024
        ),
        name="layer",
    )(
        queries, keys, values, rates.reshape(1, count),
        w_one[0], w_three[0], w_two[0], gain.reshape(1, width), order,
    )


def solution(mesh):
    in_specs = (
        P("cam", "head"),
        P("cam", "head"),
        P("cam", "head"),
        P("cam", "head"),
        P("head", None, None),
        P("head", None, None),
        P("head", None, None),
        P("head"),
        P("cam", None),
    )
    step = functools.partial(per_device, mesh.shape["cam"], mesh.shape["head"])
    return jax.shard_map(
        step, mesh=mesh, in_specs=in_specs, out_specs=P("cam", "head"), check_vma=False
    )
```

```python
import functools
import jax
import jax.numpy as jnp
from jax import lax
from jax.experimental import pallas as pl
from jax.experimental.pallas import tpu as pltpu
from jax.sharding import PartitionSpec as P

PATCHES = 32
EPSILON = 1e-06
GROUP = 8
PLANE = 4
MESH = pl.DeviceIdType.MESH
F32 = jnp.float32
BF16 = jnp.bfloat16


def nt(a, b):
    return lax.dot_general(a, b, (((1,), (1,)), ((), ())), preferred_element_type=F32)


def nn(a, b):
    return jnp.dot(a, b, preferred_element_type=F32)


def column_of(row):
    return jnp.transpose(jnp.broadcast_to(row, (128, 128)))


def drain(ref, sem):
    pltpu.make_async_copy(ref, ref, sem).wait()


def mean_square(weight):
    wf = weight.astype(F32)
    return jnp.mean(wf * wf)


def renewed(rows, grad, weight_square, grad_square):
    scale = jnp.sqrt(weight_square) / jnp.sqrt(grad_square + EPSILON)
    moved = rows - scale * grad
    ratio = jnp.sqrt(jnp.sum(rows * rows, axis=1, keepdims=True)) / jnp.sqrt(
        jnp.sum(moved * moved, axis=1, keepdims=True) + EPSILON
    )
    return moved * ratio


def layer(
    cams, heads,
    q_hbm, k_hbm, v_hbm, rates_hbm, w1_hbm, w3_hbm, w2_hbm, gain_hbm, order_hbm,
    out_ref,
    q_ref, k_ref, v_ref, rates_ref, w1_ref, w3_ref, w2_ref, gain_ref, order_ref,
    acc, pick_b, w32, line_own, sums_own, sums_in, sbuf, rbuf, obuf, ret, gbuf, gall, plane_in, line_in, u_buf, y_buf,
    rcol, ocol, sq_own, sq_in,
    bulk_send, bulk_recv, back_send, back_recv,
    g_send, g_recv, sq_send, sq_recv, in_sem, sums_send, sums_recv,
):
    count, width = q_ref.shape
    lines = cams // PLANE
    blocks = cams // GROUP
    rows = GROUP * PATCHES
    frame_rows = cams * PATCHES
    hid = w1_ref.shape[0]
    plane_rows = hid // PLANE
    line_rows = plane_rows // lines
    cam = lax.axis_index("cam")
    head = lax.axis_index("head")
    line, place = cam // PLANE, cam % PLANE

    def load(n, src, dst):
        copy = pltpu.make_async_copy(src, dst, in_sem.at[n])
        copy.start()
        return copy

    early = [
        load(n, src, dst)
        for n, (src, dst) in enumerate(
            ((order_hbm, order_ref), (q_hbm, q_ref), (k_hbm, k_ref), (v_hbm, v_ref))
        )
    ]
    barrier = pltpu.get_barrier_semaphore()

    def greet_cam(o, c):
        peer = (cam + cams // 2 + o) % cams
        pl.semaphore_signal(barrier, inc=1, device_id=(peer, head), device_id_type=MESH)
        return c

    def greet_head(o, c):
        pl.semaphore_signal(
            barrier, inc=1, device_id=(cam, (head + o) % heads), device_id_type=MESH
        )
        return c

    lax.fori_loop(0, cams // 2, greet_cam, 0)
    lax.fori_loop(cams // 2 + 1, cams, greet_cam, 0)
    lax.fori_loop(1, heads, greet_head, 0)

    later = [
        load(n + 4, src, dst)
        for n, (src, dst) in enumerate(
            (
                (rates_hbm, rates_ref), (w1_hbm, w1_ref), (w3_hbm, w3_ref),
                (w2_hbm, w2_ref), (gain_hbm, gain_ref),
            )
        )
    ]

    def block_at(turn):
        return (cam // GROUP + turn) % blocks

    def sort_block(frame, turn, arriving=(None, None, None)):
        blk = block_at(turn)
        first = frame * frame_rows + blk * rows
        slot = lax.broadcasted_iota(jnp.int32, (rows, count), 0) + first
        pick = jnp.where(slot == order_ref[...], 1.0, 0.0).astype(BF16)
        for a, ref in enumerate((q_ref, k_ref, v_ref)):
            if arriving[a] is not None:
                arriving[a].wait()
            got = nn(pick, ref[...]).astype(BF16).reshape(GROUP, PATCHES, width)
            sbuf[frame, pl.ds(blk * GROUP, GROUP), a] = got

    def send_block(frame, turn, half=None):
        blk = block_at(turn)
        low = 1 if turn == 0 else 0
        low, high = {None: (low, GROUP), 0: (low, GROUP // 2), 1: (GROUP // 2, GROUP)}[half]

        def one(j, c):
            dest = blk * GROUP + (cam + j) % GROUP
            pltpu.make_async_remote_copy(
                src_ref=sbuf.at[frame, dest],
                dst_ref=rbuf.at[frame, cam],
                send_sem=bulk_send.at[frame],
                recv_sem=bulk_recv.at[frame],
                device_id=(dest, head),
                device_id_type=MESH,
            ).start()
            return c

        if turn == 0 and half != 1:
            pltpu.make_async_copy(
                sbuf.at[frame, cam], rbuf.at[frame, cam], bulk_recv.at[frame]
            ).start()
        lax.fori_loop(low, high, one, 0)

    def attend_block(frame, turn):
        blk = block_at(turn)
        query = rbuf[frame, pl.ds(blk * GROUP, GROUP), 0].reshape(rows, width)
        key = rbuf[frame, :, 1].reshape(frame_rows, width)
        value = rbuf[frame, :, 2].reshape(frame_rows, width)
        scores = nt(query, key) * (width ** (-0.5))
        expo = jnp.exp(scores - jnp.max(scores, axis=1, keepdims=True))
        probs = (expo * (1.0 / jnp.sum(expo, axis=1, keepdims=True))).astype(BF16)
        got = nn(probs, value).astype(BF16).reshape(GROUP, PATCHES, width)
        obuf[frame, pl.ds(blk * GROUP, GROUP)] = got

    def return_block(frame, turn):
        blk = block_at(turn)

        def one(j, c):
            dest = blk * GROUP + (cam + j) % GROUP
            pltpu.make_async_remote_copy(
                src_ref=obuf.at[frame, dest],
                dst_ref=ret.at[frame, cam],
                send_sem=back_send.at[frame],
                recv_sem=back_recv.at[frame, turn],
                device_id=(dest, head),
                device_id_type=MESH,
            ).start()
            return c

        if turn == 0:
            pltpu.make_async_copy(
                obuf.at[frame, cam], ret.at[frame, cam], back_recv.at[frame, turn]
            ).start()
        lax.fori_loop(1 if turn == 0 else 0, GROUP, one, 0)

    turns = [t for t in (2, 1, 3, 0) if t < blocks]

    def columns(b, c):
        lanes = pl.ds(pl.multiple_of(b * 128, 128), 128)
        here = pl.ds(pl.multiple_of(b * 128, 128), 128)
        rcol[here] = column_of(rates_ref[:, lanes])
        ocol[here] = column_of(order_ref[:, lanes].astype(F32))
        return c

    def grad_step(i, c):
        step = 512
        here = pl.ds(pl.multiple_of(i * step, step), step)
        key, val = k_ref[here], v_ref[here].astype(F32)
        rate = rcol[here]
        err = (-jnp.concatenate([rate, rate], axis=1) * val).astype(BF16)
        a1, a3 = nt(w1_ref[...], key), nt(w3_ref[...], key)
        s = jax.nn.sigmoid(a1)
        act = (a1 * s * a3).astype(BF16)
        back = nt(u_buf[0], err)
        b1 = (back * a3 * s * (1.0 + a1 * (1.0 - s))).astype(BF16)
        b3 = (back * a1 * s).astype(BF16)
        gbuf[0] += nn(b1, key)
        gbuf[1] += nn(b3, key)
        gbuf[2] += nn(act, err)
        return c

    def pick_of(frame, here, step):
        at = ocol[here]
        lane = lax.broadcasted_iota(jnp.int32, (step, 128), 1).astype(F32)
        return jnp.concatenate(
            [
                jnp.where(at == lane + float(frame * frame_rows + b), 1.0, 0.0).astype(BF16)
                for b in range(0, frame_rows, 128)
            ],
            axis=1,
        )

    def build_pick(i, c):
        here = pl.ds(pl.multiple_of(i * 256, 256), 256)
        pick = pick_of(1, here, 256)
        for b in range(blocks):
            pick_b[b, here] = pick[:, b * rows : (b + 1) * rows]
        return c

    def plane_peer(o):
        return (line * PLANE + (place + o) % PLANE, head)

    def line_peer(o):
        return (((line + o) % lines) * PLANE + place, head)

    def stage(n, src, dst, peer):
        pltpu.make_async_remote_copy(
            src_ref=src, dst_ref=dst, send_sem=g_send.at[n], recv_sem=g_recv.at[n],
            device_id=peer, device_id_type=MESH,
        ).start()

    far, sides, near = turns[:1], turns[1:-1], turns[-1:]
    if len(turns) == 1:
        far, near = turns, []

    early[0].wait()
    for t in far:
        sort_block(0, t, early[1:])
    pl.semaphore_wait(barrier, cams - 1 + heads - 1)
    for t in far:
        send_block(0, t)

    for copy in later:
        copy.wait()
    lax.fori_loop(0, count // 128, columns, 0)
    for m, w in enumerate((w1_ref, w3_ref, w2_ref)):
        w32[m] = w[...].astype(F32)
    u_buf[0] = jnp.transpose(w32[2]).astype(BF16)
    gbuf[...] = jnp.zeros_like(gbuf)
    lax.fori_loop(0, count // 512, grad_step, 0)
    gbuf[2] = jnp.transpose(gbuf[2])
    for t in sides[:1]:
        sort_block(0, t)
    for o in range(1, PLANE):
        theirs = pl.ds(((place + o) % PLANE) * plane_rows, plane_rows)
        stage(0, gbuf.at[:, theirs], plane_in.at[o - 1], plane_peer(o))
    for t in sides[1:]:
        sort_block(0, t)
    for t in sides:
        send_block(0, t, 0)
    for t in near:
        sort_block(0, t)
    for t in near:
        send_block(0, t)
    for t in far + sides[:1]:
        sort_block(1, t)
    drain(plane_in, g_recv.at[0])
    drain(plane_in, g_send.at[0])
    mine = pl.ds(place * plane_rows, plane_rows)
    gbuf[:, mine] += plane_in[0] + plane_in[1] + plane_in[2]

    for o in range(1, lines):
        theirs = pl.ds(place * plane_rows + ((line + o) % lines) * line_rows, line_rows)
        stage(1, gbuf.at[:, theirs], line_in.at[o - 1], line_peer(o))
    for t in sides:
        send_block(0, t, 1)
    for t in far:
        send_block(1, t, 0)
    for t in sides[1:] + near:
        sort_block(1, t)
    drain(line_in, g_recv.at[1])
    drain(line_in, g_send.at[1])
    own = pl.ds(place * plane_rows + line * line_rows, line_rows)
    total = gbuf[:, own]
    for o in range(1, lines):
        total = total + line_in[o - 1]
    lane = lax.broadcasted_iota(jnp.int32, (1, 128), 1)
    squares = jnp.zeros((1, 128), F32)
    for m in range(3):
        squares = jnp.where(lane == m, jnp.sum(total[m] * total[m]), squares)
    sums_own[...] = squares
    line_own[...] = total

    def send_sums(o, c):
        pltpu.make_async_remote_copy(
            src_ref=sums_own, dst_ref=sums_in.at[o - 1],
            send_sem=sums_send, recv_sem=sums_recv,
            device_id=((cam + o) % cams, head), device_id_type=MESH,
        ).start()
        return c

    lax.fori_loop(1, cams, send_sums, 0)
    for t in far:
        send_block(1, t, 1)
    for t in sides:
        send_block(1, t, 0)
    drain(rbuf.at[0], bulk_recv.at[0])
    for t in turns:
        attend_block(0, t)
    weight_squares = [mean_square(w[...]) for w in (w1_ref, w3_ref, w2_ref)]
    drain(sums_in, sums_recv)
    drain(sums_in, sums_send)
    squares = sums_own[...] + jnp.sum(sums_in[...], axis=0)
    for m, w in enumerate((w1_ref, w3_ref, w2_ref)):
        square = jnp.sum(jnp.where(lane == m, squares, 0.0)) / (hid * width)
        piece = renewed(w32[m, own], line_own[m], weight_squares[m], square)
        gall[place, line, m] = jnp.concatenate(
            [piece[:, :128], piece[:, 128:]], axis=0
        ).astype(BF16)

    for o in range(1, lines):
        stage(2, gall.at[place, line], gall.at[place, line], line_peer(o))
    for t in sides:
        send_block(1, t, 1)
    for t in near:
        send_block(1, t)
    for t in turns:
        return_block(0, t)
    drain(gall.at[0, pl.ds(0, lines - 1)], g_recv.at[2])
    drain(gall.at[0, pl.ds(0, lines - 1)], g_send.at[2])
    for o in range(1, PLANE):
        stage(3, gall.at[place], gall.at[place], plane_peer(o))
    lax.fori_loop(0, count // 256, build_pick, 0)

    drain(rbuf.at[1], bulk_recv.at[1])
    attend_block(1, turns[0])
    for a, b in zip(turns[1:], turns[:-1]):
        attend_block(1, a)
        return_block(1, b)
    return_block(1, turns[-1])

    drain(gall.at[pl.ds(0, PLANE - 1)], g_recv.at[3])
    drain(gall.at[pl.ds(0, PLANE - 1)], g_send.at[3])
    for m in range(3):
        for p in range(PLANE):
            for n in range(lines):
                at = pl.ds(p * plane_rows + n * line_rows, line_rows)
                piece = gall[p, n, m].astype(F32)
                gbuf[m, at] = jnp.concatenate([piece[:line_rows], piece[line_rows:]], axis=1)
    u_buf[...] = gbuf[...].astype(BF16)

    def readout(i, c):
        step = 256
        here = pl.ds(pl.multiple_of(i * step, step), step)
        query = q_ref[here]
        q1, q3 = nt(query, u_buf[0]), nt(query, u_buf[1])
        act = (q1 * jax.nn.sigmoid(q1) * q3).astype(BF16)
        y = nt(act, u_buf[2])
        y_buf[here] = y * gain_ref[...]
        half = y[:, :128] * y[:, :128] + y[:, 128:] * y[:, 128:]
        for b in range(step // 128):
            part = jnp.sum(jnp.transpose(half[b * 128 : (b + 1) * 128]), axis=0, keepdims=True)
            sq_own[pl.ds(i * (step // 128) + b, 1)] = part
        return c

    lax.fori_loop(0, count // 256, readout, 0)

    def send_sq(o, c):
        pltpu.make_async_remote_copy(
            src_ref=sq_own, dst_ref=sq_in.at[o - 1], send_sem=sq_send, recv_sem=sq_recv,
            device_id=(cam, (head + o) % heads), device_id_type=MESH,
        ).start()
        return c

    lax.fori_loop(1, heads, send_sq, 0)

    def owners_at(turn):
        return (cam // GROUP - turn) % blocks

    def await_return(frame, turn):
        drain(ret.at[frame, pl.ds(owners_at(turn) * GROUP, GROUP)], back_recv.at[frame, turn])

    for t in turns:
        await_return(0, t)

    def first_half(i, c):
        here = pl.ds(pl.multiple_of(i * 256, 256), 256)
        acc[here] = nn(pick_of(0, here, 256), ret[0].reshape(frame_rows, width))
        return c

    lax.fori_loop(0, count // 256, first_half, 0)

    drain(sq_in, sq_send)
    drain(sq_in, sq_recv)
    square = sq_own[...]
    for o in range(1, heads):
        square = square + sq_in[o - 1]
    sq_own[...] = 1.0 / jnp.sqrt(square / (width * heads) + EPSILON)

    def scaled(b, c):
        here = pl.ds(pl.multiple_of(b * 128, 128), 128)
        rcol[here] = column_of(sq_own[pl.ds(b, 1)])
        return c

    lax.fori_loop(0, count // 128, scaled, 0)

    for t in turns:
        await_return(1, t)

    tail = min(count, 1024)

    def second_half(i, c):
        here = pl.ds(pl.multiple_of(i * tail, tail), tail)
        inv = rcol[here]
        got = acc[here] + y_buf[here] * jnp.concatenate([inv, inv], axis=1)
        for b in range(blocks):
            got += nn(pick_b[b, here], ret[1, b * GROUP : (b + 1) * GROUP].reshape(rows, width))
        out_ref[here] = got.astype(BF16)
        return c

    lax.fori_loop(0, count // tail, second_half, 0)
    for frame in range(2):
        drain(sbuf.at[frame, pl.ds(0, cams - 1)], bulk_send.at[frame])
        drain(obuf.at[frame, pl.ds(0, cams - 1)], back_send.at[frame])


def per_device(cams, heads, queries, keys, values, rates, w_one, w_three, w_two, gain, order):
    count, width = queries.shape
    hid = w_one.shape[1]
    plane_rows = hid // PLANE
    lines = cams // PLANE
    line_rows = plane_rows // lines
    dma = pltpu.SemaphoreType.DMA
    hbm = pl.BlockSpec(memory_space=pl.ANY)
    return pl.pallas_call(
        functools.partial(layer, cams, heads),
        out_shape=pltpu.VMEM((count, width), BF16),
        in_specs=[hbm] * 9,
        out_specs=pl.BlockSpec(memory_space=pltpu.VMEM),
        scratch_shapes=[
            pltpu.VMEM((count, width), BF16),
            pltpu.VMEM((count, width), BF16),
            pltpu.VMEM((count, width), BF16),
            pltpu.VMEM((1, count), F32),
            pltpu.VMEM((hid, width), BF16),
            pltpu.VMEM((hid, width), BF16),
            pltpu.VMEM((width, hid), BF16),
            pltpu.VMEM((1, width), F32),
            pltpu.VMEM((1, count), jnp.int32),
            pltpu.VMEM((count, width), F32),
            pltpu.VMEM((cams // GROUP, count, GROUP * PATCHES), BF16),
            pltpu.VMEM((3, hid, width), F32),
            pltpu.VMEM((3, line_rows, width), F32),
            pltpu.VMEM((1, 128), F32),
            pltpu.VMEM((cams - 1, 1, 128), F32),
            pltpu.VMEM((2, cams, 3, PATCHES, width), BF16),
            pltpu.VMEM((2, cams, 3, PATCHES, width), BF16),
            pltpu.VMEM((2, cams, PATCHES, width), BF16),
            pltpu.VMEM((2, cams, PATCHES, width), BF16),
            pltpu.VMEM((3, hid, width), F32),
            pltpu.VMEM((PLANE, lines, 3, 2 * line_rows, width // 2), BF16),
            pltpu.VMEM((PLANE - 1, 3, plane_rows, width), F32),
            pltpu.VMEM((lines - 1, 3, line_rows, width), F32),
            pltpu.VMEM((3, hid, width), BF16),
            pltpu.VMEM((count, width), F32),
            pltpu.VMEM((count, 128), F32),
            pltpu.VMEM((count, 128), F32),
            pltpu.VMEM((count // 128, 128), F32),
            pltpu.VMEM((heads - 1, count // 128, 128), F32),
            dma((2,)),
            dma((2,)),
            dma((2,)),
            dma((2, cams // GROUP)),
            dma((4,)),
            dma((4,)),
            dma,
            dma,
            dma((9,)),
            dma,
            dma,
        ],
        compiler_params=pltpu.CompilerParams(
            collective_id=0, has_side_effects=True, vmem_limit_bytes=60 * 1024 * 1024
        ),
        name="layer",
    )(
        queries, keys, values, rates.reshape(1, count),
        w_one[0], w_three[0], w_two[0], gain.reshape(1, width), order,
    )


def solution(mesh):
    in_specs = (
        P("cam", "head"),
        P("cam", "head"),
        P("cam", "head"),
        P("cam", "head"),
        P("head", None, None),
        P("head", None, None),
        P("head", None, None),
        P("head"),
        P("cam", None),
    )
    step = functools.partial(per_device, mesh.shape["cam"], mesh.shape["head"])
    return jax.shard_map(
        step, mesh=mesh, in_specs=in_specs, out_specs=P("cam", "head"), check_vma=False
    )
```
